32 devices in a mesh: tile: 8 (over y, x, core), epoch: 4 (over z).
Axes of the slice: x: 2, y: 2, z: 4, core: 2. Of those that a mesh axis runs over, the one named last changes fastest.
Arguments:
- residual: bfloat16 [8, 128, 64, 128], P('tile', 'epoch'), may hold values from -6 to 6
- inv_variance: float32 [8, 128, 64, 128], P('tile', 'epoch'), may hold values from 0.25 to 4
- psf_coeff: float32 [8, 128, 16], P('tile', 'epoch'), may hold values from -5 to 5
- psf_taps: float32 [16, 2, 25], replicated, may hold values from -1.25 to 1.25
- patch_owner: int32 [8, 128, 1], P('tile', 'epoch'), may hold values from 0 to 3; in each aligned block of 32 rows (0 to 31, 32 to 63, ..., all dimensions but the last counted through in order) at most 16 rows name the same one
- patch_slot: int32 [8, 128], P('tile', 'epoch'), may hold values from 0 to 7
- band_id: int32 [8, 128], P('tile', 'epoch'), may hold values from 0 to 5
- tile_offset: int32 [8, 128], P('tile', 'epoch'), may hold values from 0 to 2
- col_shift: int32 [8, 128], P('tile', 'epoch'), may hold values from 0 to 7
Outputs:
- scene_adjoint: float32 [8, 6, 32, 64, 128], P('tile', None, 'epoch')
The draws below stay inside these ranges and needn't reach their ends.
Inputs may be any that keep to these rules, and one draw needn't show every extreme that they name: Among the 32 blocks of one device at most 16 have the same patch_owner, and in every draw some owner receives exactly 16 from some device.
All inputs are finite; a program needn't handle non-finite values.
Results may differ from the reference program's by a relative error of at most 0.0003.
Values sent between devices are 32-bit elements; how exact they have to be, the bound alone decides.
No kernel may reach another device: no remote copies, remote signals or barrier semaphores. Data moves between devices by JAX's collectives and lax.ppermute only.
A program may use at most 64 MiB of HBM per device.

```python
import math
import jax
import jax.numpy as jnp
import numpy as np
from jax import lax

ROWS = 64
COLS = 128
COMPS = 16
TAPS = 25
BANDS = 6
SHIFTS = 8
PATCHES = 32
E_DEV = 32
CAP = 16
PATCH_DEV = 8
BLOCKS_TILE = 128
N_TILE = 8
N_EPOCH = 4


def place_ends(drawn, stream_key, smallest, high):
    longest = drawn.shape.index(max(drawn.shape))
    spots = []
    for shift in (0, 1):
        where = [jax.random.randint(jax.random.fold_in(stream_key, axis), (), 0, length) for axis, length in enumerate(drawn.shape)]
        where[longest] = (where[longest] + shift) % drawn.shape[longest]
        spots.append(tuple(where))
    return drawn.at[spots[0]].set(smallest).at[spots[1]].set(high)


def shard_levels(stream_key, extent, shards, least, high):
    def one(dim, parts):
        heights = jax.random.uniform(jax.random.fold_in(jax.random.fold_in(stream_key, 6), dim), (parts,), jnp.float32, least / len(shards), high / len(shards))
        return jnp.repeat(jnp.exp(heights), extent[dim] // parts).reshape((-1,) + (1,) * (len(extent) - dim - 1))

    level = one(*shards[0])
    for cut in shards[1:]:
        level = level * one(*cut)
    return level


def assign_block(key, own, number, rows, number_of, top, reach, lean):
    ranking = jax.random.permutation(key, number_of)
    packed, common = load_shares(number_of, rows * top, reach, lean, True), load_shares(number_of, rows * top, reach, lean, False)
    places = jnp.arange(number_of)

    def named(tallies, turn):
        used = int((tallies > 0).sum())
        fixed = max(1, used // 4)
        shifted = fixed + (places - fixed + turn * (used - fixed)) % max(1, number_of - fixed)
        return jnp.zeros((number_of,), jnp.int32).at[ranking[jnp.where(places < fixed, places, shifted)]].set(jnp.asarray(tallies, jnp.int32))

    tallies = jnp.where(number % 4 == 0, named(packed, number // 4), named(common, number - number // 4 - 1))
    mixed = jax.random.permutation(jax.random.fold_in(own, 3), number_of)
    giver, receiver = mixed[0:number_of // 2 * 2:2], mixed[1:number_of // 2 * 2:2]
    margin = jnp.minimum(tallies[giver] - 1, reach - tallies[receiver]) // 2
    margin = jnp.where((giver == ranking[0]) | (receiver == ranking[0]) | (tallies[receiver] == 0), 0, jnp.maximum(margin, 0))
    shifted = jax.random.randint(jax.random.fold_in(own, 4), (number_of // 2,), 0, 1 << 20) % (margin + 1)
    tallies = tallies.at[giver].add(-shifted).at[receiver].add(shifted)
    labels = jnp.searchsorted(jnp.cumsum(tallies), jnp.arange(rows * top), side="right").astype(jnp.int32)
    table = labels.reshape(top, rows).T
    table = table[jax.random.permutation(jax.random.fold_in(own, 1), rows)]
    turn = jax.random.randint(jax.random.fold_in(own, 2), (rows, 1), 0, top)
    return jnp.take_along_axis(table, (jnp.arange(top)[None, :] + turn) % top, axis=1)


def load_shares(number_of, total, limit, lean, full):
    weights = [(1 << 20) // math.isqrt(standing ** lean) + 1 for standing in range(1, number_of + 1)]
    largest = limit if full else min(limit, max(-(-total // number_of), total * weights[0] // sum(weights)))
    least = 1 if total - largest >= number_of - 1 else 0
    holding, rest = [largest] + [least] * (number_of - 1), total - largest - least * (number_of - 1)
    while rest > 0:
        movable = [i for i in range(1, number_of) if holding[i] < largest] or [i for i in range(1, number_of) if holding[i] < limit]
        whole, remaining = sum([weights[i] for i in movable]), rest
        for i in movable:
            extra = min(limit - holding[i], max(1, remaining * weights[i] // whole), rest)
            holding[i] = holding[i] + extra
            rest = rest - extra
    return np.array(holding)


def noise(rng, extent, spread, bound, split=(), kind=jnp.bfloat16):
    factor_of = shard_levels(rng, extent, split, -0.22, 0.18) if split else 1.0
    values = jax.random.normal(rng, extent, jnp.float32) * spread * factor_of
    return jnp.minimum(jnp.maximum(values, -bound), bound).astype(kind)


def setup_inputs(seed: int = 0) -> dict:
    keys = jax.random.split(jax.random.key(seed), 10)
    residual = noise(keys[0], (N_TILE, BLOCKS_TILE, ROWS, COLS), 1.0, 6.0, ((0, 8), (1, 4)))
    inv_variance = jnp.clip(jnp.exp(math.log(4.0) - 2.7725887 * jax.random.uniform(keys[1], (N_TILE, BLOCKS_TILE, ROWS, COLS), jnp.float32) ** shard_levels(keys[1], (N_TILE, BLOCKS_TILE, ROWS, COLS), ((0, 8), (1, 4)), -0.2, 0.2)), 0.25, 4.0)
    psf_coeff = noise(keys[2], (N_TILE, BLOCKS_TILE, COMPS), 1.0, 5.0, ((0, 8), (1, 4)), jnp.float32)
    psf_taps = noise(keys[3], (COMPS, 2, TAPS), TAPS ** -0.5, 1.25, (), jnp.float32)
    patch_owner_keys = jax.random.split(jax.random.fold_in(keys[4], 1), N_TILE * BLOCKS_TILE // E_DEV)
    patch_owner_turns = jax.random.permutation(jax.random.fold_in(keys[4], 3), N_TILE * BLOCKS_TILE // E_DEV)
    patch_owner = jax.vmap(lambda own, number: assign_block(jax.random.fold_in(keys[4], 2), own, number, E_DEV, N_EPOCH, 1, CAP, 2))(patch_owner_keys, patch_owner_turns).reshape((N_TILE, BLOCKS_TILE, 1))
    patch_slot = place_ends(jax.random.randint(keys[5], (N_TILE, BLOCKS_TILE), 0, PATCH_DEV), jax.random.fold_in(keys[5], 1), 0, PATCH_DEV - 1).astype(jnp.int32)
    band_id = place_ends(jax.random.randint(keys[6], (N_TILE, BLOCKS_TILE), 0, BANDS), jax.random.fold_in(keys[6], 1), 0, BANDS - 1).astype(jnp.int32)
    tile_offset = place_ends(jax.random.randint(keys[7], (N_TILE, BLOCKS_TILE), 0, 3), jax.random.fold_in(keys[7], 1), 0, 2).astype(jnp.int32)
    col_shift = place_ends(jax.random.randint(keys[8], (N_TILE, BLOCKS_TILE), 0, SHIFTS), jax.random.fold_in(keys[8], 1), 0, SHIFTS - 1).astype(jnp.int32)
    return {"residual": residual, "inv_variance": inv_variance, "psf_coeff": psf_coeff, "psf_taps": psf_taps, "patch_owner": patch_owner, "patch_slot": patch_slot, "band_id": band_id, "tile_offset": tile_offset, "col_shift": col_shift}


def band_matrix(taps_row, size):
    index = jnp.arange(size)
    offsets = index[:, None] - index[None, :] + (taps_row.shape[1] - 1) // 2
    select = (offsets[None, :, :] == jnp.arange(taps_row.shape[1])[:, None, None]).astype(jnp.float32)
    return jnp.einsum('kij,ck->cij', select, taps_row, precision=lax.Precision.HIGHEST)


def block_images(residual, inv_variance, psf_coeff, col_shift, colmat, rowmat):
    count = residual.shape[0]
    weighted = inv_variance * residual.astype(jnp.float32)
    flat_cols = jnp.transpose(colmat, (1, 0, 2)).reshape(COLS, COMPS * COLS)
    across = jnp.dot(weighted.reshape(count * ROWS, COLS), flat_cols, precision=lax.Precision.HIGHEST)
    across = across.reshape(count, ROWS, COMPS, COLS) * psf_coeff[:, None, :, None]
    image = jnp.einsum('kir,eikd->erd', rowmat, across, precision=lax.Precision.HIGHEST)
    index = jnp.arange(COLS)
    shifter = (index[None, None, :] == index[None, :, None] + col_shift[:, None, None]).astype(jnp.float32)
    return jnp.einsum('eri,eij->erj', image, shifter, precision=lax.Precision.HIGHEST)


def reference(residual, inv_variance, psf_coeff, psf_taps, patch_owner, patch_slot, band_id, tile_offset, col_shift):
    colmat = band_matrix(psf_taps[:, 0], COLS)
    rowmat = band_matrix(psf_taps[:, 1], ROWS)

    def one_group(args):
        res, wts, coef, shift = args
        return block_images(res, wts, coef, shift, colmat, rowmat)

    images = lax.map(one_group, (residual, inv_variance, psf_coeff, col_shift))
    groups = jnp.arange(N_TILE, dtype=jnp.int32)[:, None]
    target = groups + tile_offset - 1
    valid = ((target >= 0) & (target < N_TILE)).astype(jnp.float32)
    target = jnp.clip(target, 0, N_TILE - 1)
    patch = patch_owner[:, :, 0] * PATCH_DEV + patch_slot
    flat_index = ((target * BANDS + band_id) * PATCHES + patch).reshape(-1).astype(jnp.int32)
    contrib = (images * valid[:, :, None, None]).reshape(-1, ROWS, COLS)
    total = jnp.zeros((N_TILE * BANDS * PATCHES, ROWS, COLS), jnp.float32)
    total = total.at[flat_index].add(contrib)
    return total.reshape(N_TILE, BANDS, PATCHES, ROWS, COLS)
```

```python
import functools
import math

import jax
import jax.numpy as jnp
from jax import lax
from jax.experimental import pallas as pl
from jax.experimental.pallas import tpu as pltpu
from jax.sharding import PartitionSpec as P

BANDS = 6
PATCHES = 32
HEAD = 8
LANES = 128


SMEM = pltpu.SMEM
VMEM = pltpu.VMEM
MIB = 1 << 20


def halves(x):
    high = x.astype(jnp.bfloat16)
    low = (x - high.astype(jnp.float32)).astype(jnp.bfloat16)
    return high, low


def plan_chunks(capacity):
    if capacity >= 16:
        sizes = (capacity // 4, capacity // 2, capacity - capacity // 4 - capacity // 2)
    else:
        sizes = (capacity // 2, capacity - capacity // 2)
    starts = [sum(sizes[:k]) for k in range(len(sizes))]
    return list(zip(starts, sizes))


def head_lanes():
    return lax.broadcasted_iota(jnp.int32, (HEAD, LANES), 1)


def build_bands(taps_ref, cols_ref, rows_ref):
    comps, _, taps = taps_ref.shape
    cols = cols_ref.shape[1] // 2
    rows = rows_ref.shape[1] // 4
    half = (taps - 1) // 2
    tap = lax.broadcasted_iota(jnp.int32, (taps, LANES), 0)
    lane = lax.broadcasted_iota(jnp.int32, (taps, LANES), 1)
    place_col = (lax.rem(lane + tap - half + cols, cols) == 0).astype(jnp.float32)
    place_row = (lax.rem(lane - tap + half + 2 * rows, rows) == 0).astype(jnp.float32)
    base_col = jnp.dot(
        taps_ref[:, 0, :], place_col, precision=lax.Precision.HIGHEST,
        preferred_element_type=jnp.float32,
    )
    base_row = jnp.dot(
        taps_ref[:, 1, :], place_row, precision=lax.Precision.HIGHEST,
        preferred_element_type=jnp.float32,
    )
    up = lax.broadcasted_iota(jnp.int32, (cols, LANES), 0)
    across = lax.broadcasted_iota(jnp.int32, (cols, LANES), 1)
    near_col = jnp.abs(across - up) <= half
    up_row = lax.broadcasted_iota(jnp.int32, (rows, LANES), 0)
    across_row = lax.rem(lax.broadcasted_iota(jnp.int32, (rows, LANES), 1), rows)
    near_row = jnp.abs(across_row - up_row) <= half
    for c in range(comps):
        wide = jnp.broadcast_to(base_col[c : c + 1, :], (cols, LANES))
        wide = pltpu.roll(wide, 0, 1, stride=1, stride_axis=0)
        high, low = halves(jnp.where(near_col, wide, 0.0))
        cols_ref[c * cols : (c + 1) * cols, :] = jnp.concatenate([high, low], axis=1)
        wide = jnp.broadcast_to(base_row[c : c + 1, :], (rows, LANES))
        wide = pltpu.roll(wide, 0, 1, stride=1, stride_axis=0)
        high, low = halves(jnp.where(near_row, wide, 0.0))
        rows_ref[c * rows : (c + 1) * rows, :] = jnp.concatenate([high, low], axis=1)


def resample_kernel(cfg, first, jobs, with_self, *refs):
    epochs, capacity, per_dev, tiles, count, rows, cols = cfg
    cells = BANDS * per_dev
    n_out = len(jobs) * (epochs - 1) + (1 if with_self else 0)
    owner_ref, slot_ref, band_ref, offset_ref, shift_ref, coeff_ref = refs[:6]
    res_hbm, inv_hbm = refs[6:8]
    taps_ref = cols_in = rows_in = None
    if first:
        taps_ref = refs[8]
        rest = refs[9:]
        outs, (cols_ref, rows_ref) = rest[:n_out], rest[n_out : n_out + 2]
        rest = rest[n_out + 2 :]
    else:
        cols_ref, rows_ref = refs[8:10]
        rest = refs[10:]
        outs = rest[:n_out]
        rest = rest[n_out:]
    res_ref, inv_ref, spread_ref, used_ref, block_ref, label_ref, todo_ref, sems = rest

    fetch_res = pltpu.make_async_copy(res_hbm, res_ref, sems.at[0])
    fetch_inv = pltpu.make_async_copy(inv_hbm, inv_ref, sems.at[1])
    fetch_res.start()
    fetch_inv.start()

    me = lax.axis_index("epoch")
    tile = lax.axis_index("tile")
    for e in range(epochs):
        used_ref[e] = 0
    for i in range(epochs * capacity):
        label_ref[i] = 0
        block_ref[i] = 0

    def place(central, b, carry):
        off = offset_ref[b]
        target = tile + off - 1
        fits = (target >= 0) & (target < tiles) & ((off == 1) == central)

        @pl.when(fits)
        def _():
            o = owner_ref[b]
            rank = used_ref[o]
            used_ref[o] = rank + 1
            at = o * capacity + rank
            block_ref[at] = b
            label_ref[at] = off * cells + band_ref[b] * per_dev + slot_ref[b] + 1

        return carry

    lax.fori_loop(0, count, functools.partial(place, False), 0)
    lax.fori_loop(0, count, functools.partial(place, True), 0)

    total = jnp.int32(0)
    parts = [(d, start, size) for start, size in jobs for d in range(1, epochs)]
    if with_self:
        parts.append((0, 0, capacity))
    for out_at, (d, start, size) in enumerate(parts):
        o = lax.rem(me + d, epochs)
        have = used_ref[o]
        for s in range(0, size, 2):
            todo_ref[0, total] = o * capacity + start + s
            todo_ref[1, total] = out_at
            todo_ref[2, total] = s
            total = total + (start + s < have).astype(jnp.int32)

    if first:
        build_bands(taps_ref, cols_ref, rows_ref)

    lane = head_lanes()
    for out_at, (d, start, size) in enumerate(parts):
        if start == 0:
            o = lax.rem(me + d, epochs)
            head = jnp.zeros((HEAD, LANES), jnp.float32)
            for j in range(capacity):
                head = jnp.where(
                    lane == j, label_ref[o * capacity + j].astype(jnp.float32), head
                )
            outs[out_at][size * rows : size * rows + HEAD, :] = head

    fetch_res.wait()
    fetch_inv.wait()
    comps = cols_ref.shape[0] // cols

    def work(i, carry):
        at = todo_ref[0, i]
        out_at = todo_ref[1, i]
        s = todo_ref[2, i]
        blocks = [block_ref[at], block_ref[jnp.minimum(at + 1, epochs * capacity - 1)]]
        sides = []
        for b in blocks:
            high, low = halves(inv_ref[b] * res_ref[b].astype(jnp.float32))
            sides.append(jnp.concatenate([high, low, high, low], axis=0))
        down = jnp.dot(
            rows_ref[...], jnp.concatenate(sides, axis=1), preferred_element_type=jnp.float32
        )
        for c in range(comps):
            for g in range(2):
                part = down[c * rows : (c + 1) * rows, g * cols : (g + 1) * cols]
                high, low = halves(part * coeff_ref[c, blocks[g]])
                spread_ref[g * rows : (g + 1) * rows, c * cols : (c + 1) * cols] = high
                spread_ref[(2 + g) * rows : (3 + g) * rows, c * cols : (c + 1) * cols] = low
        both = jnp.dot(spread_ref[...], cols_ref[...], preferred_element_type=jnp.float32)
        lanes = lax.broadcasted_iota(jnp.int32, (rows, cols), 1)
        for g in range(2):
            high = both[g * rows : (g + 1) * rows]
            low = both[(2 + g) * rows : (3 + g) * rows]
            image = high[:, :cols] + (high[:, cols:] + low[:, :cols])
            shift = shift_ref[blocks[g]]
            image = jnp.where(lanes >= shift, pltpu.roll(image, shift, 1), 0.0)
            for k, (d, start, size) in enumerate(parts):
                last = size % 2 == 1

                @pl.when((out_at == k) & ((s + g < size) if last else True))
                def _():
                    outs[k][pl.ds(pl.multiple_of((s + g) * rows, rows), rows), :] = image

        return carry

    lax.fori_loop(0, total, work, 0)


def read_heads(sources, head_refs, sems):
    copies = [
        pltpu.make_async_copy(src.at[pl.ds(src.shape[0] - HEAD, 1)], dst, sems.at[i])
        for i, (src, dst) in enumerate(zip(sources, head_refs))
    ]
    for copy in copies:
        copy.start()
    for copy in copies:
        copy.wait()


def collect_kernel(cfg, chunks, k, sends, *refs):
    epochs, capacity, per_dev, tiles, count, rows, cols = cfg
    cells = BANDS * per_dev
    n = epochs - 1
    at = 0
    if k > 0:
        table_ref, state_ref, total_in = refs[:3]
        at = 3
    own_ref = refs[at]
    at += 1
    arrived = []
    for kk in range(k + 1):
        arrived.append(refs[at : at + n])
        at += n
    total_ref, next_ref, prev_ref = refs[at : at + 3]
    at += 3
    if k == 0:
        table_out = refs[at]
        at += 1
    state_out = refs[at]
    at += 1
    if k == 0:
        head_refs = refs[at : at + epochs]
        sems = refs[at + epochs]
        sources = [own_ref, *arrived[0]]
        read_heads(sources, head_refs, sems)
        for d in range(epochs):

            def copy_label(j, carry, d=d):
                table_out[d * capacity + j] = head_refs[d][0, j].astype(jnp.int32)
                return carry

            lax.fori_loop(0, capacity, copy_label, 0)
        table_ref = table_out
        total_ref[...] = jnp.zeros_like(total_ref)
        sent = [jnp.int32(0), jnp.int32(0)]
    else:
        total_ref[...] = total_in[...]
        sent = [state_ref[0], state_ref[1]]
    lane = head_lanes()
    cap = sends[k]

    def scan(src, d, first_slot, base, slots, fresh, carry):
        def step(j, carry):
            queued_next, queued_prev, head_next, head_prev = carry
            label = table_ref[d * capacity + base + j] - 1
            block = pl.ds(pl.multiple_of((first_slot + j) * rows, rows), rows)
            if fresh:

                @pl.when((label >= cells) & (label < 2 * cells))
                def _():
                    cell = label - cells
                    total_ref[cell] = total_ref[cell] + src[block, :]

            up = label >= 2 * cells
            down = (label >= 0) & (label < cells)
            place_next = queued_next - sent[0]
            place_prev = queued_prev - sent[1]
            put_next = up & (place_next >= 0) & (place_next < cap)
            put_prev = down & (place_prev >= 0) & (place_prev < cap)

            @pl.when(put_next)
            def _():
                next_ref[pl.ds(pl.multiple_of(place_next * rows, rows), rows), :] = src[block, :]

            @pl.when(put_prev)
            def _():
                prev_ref[pl.ds(pl.multiple_of(place_prev * rows, rows), rows), :] = src[block, :]

            mark_next = jnp.where(put_next, place_next, -1)
            mark_prev = jnp.where(put_prev, place_prev, -1)
            head_next = jnp.where(
                lane == mark_next, (label - 2 * cells + 1).astype(jnp.float32), head_next
            )
            head_prev = jnp.where(lane == mark_prev, (label + 1).astype(jnp.float32), head_prev)
            return (
                queued_next + up.astype(jnp.int32),
                queued_prev + down.astype(jnp.int32),
                head_next,
                head_prev,
            )

        return lax.fori_loop(0, slots, step, carry)

    blank = jnp.zeros((HEAD, LANES), jnp.float32)
    carry = (jnp.int32(0), jnp.int32(0), blank, blank)
    for kk in range(k + 1):
        if kk == 0:
            carry = scan(own_ref, 0, 0, 0, capacity, k == 0, carry)
        start, size = chunks[kk]
        for d in range(1, epochs):
            carry = scan(arrived[kk][d - 1], d, 0, start, size, kk == k, carry)
    queued_next, queued_prev, head_next, head_prev = carry
    next_ref[cap * rows : cap * rows + HEAD, :] = head_next
    prev_ref[cap * rows : cap * rows + HEAD, :] = head_prev
    state_out[0] = jnp.minimum(sent[0] + cap, queued_next)
    state_out[1] = jnp.minimum(sent[1] + cap, queued_prev)


def finish_kernel(rows, *refs):
    total_ref = refs[0]
    waves = (len(refs) - 3) // 2
    sources = refs[1 : 1 + waves]
    out_ref = refs[1 + waves]
    head_refs = refs[2 + waves : 2 + 2 * waves]
    sems = refs[2 + 2 * waves]
    read_heads(sources, head_refs, sems)
    out_ref[...] = total_ref[...]
    for src, head in zip(sources, head_refs):

        def step(j, carry, src=src, head=head):
            cell = head[0, j].astype(jnp.int32) - 1

            @pl.when(cell >= 0)
            def _():
                block = pl.ds(pl.multiple_of(j * rows, rows), rows)
                out_ref[cell] = out_ref[cell] + src[block, :]

            return carry

        lax.fori_loop(0, (src.shape[0] - HEAD) // rows, step, 0)


def on_device(
    tiles,
    epochs,
    residual,
    inv_variance,
    psf_coeff,
    psf_taps,
    patch_owner,
    patch_slot,
    band_id,
    tile_offset,
    col_shift,
):
    count, rows, cols = residual.shape[1:]
    comps = psf_taps.shape[0]
    capacity = max(2, min(count // 2, 64 // epochs))
    per_dev = PATCHES // epochs
    cells = BANDS * per_dev
    cfg = (epochs, capacity, per_dev, tiles, count, rows, cols)
    chunks = plan_chunks(capacity)
    n = epochs - 1
    f32 = jnp.float32
    smem = pl.BlockSpec(memory_space=SMEM)
    vmem = pl.BlockSpec(memory_space=VMEM)
    hbm = pl.BlockSpec(memory_space=pl.ANY)

    def slab(slots):
        return jax.ShapeDtypeStruct((slots * rows + HEAD, cols), f32)

    scalars = (
        patch_owner.reshape(count),
        patch_slot.reshape(count),
        band_id.reshape(count),
        tile_offset.reshape(count),
        col_shift.reshape(count),
        psf_coeff[0].T,
    )
    blocks = (residual[0], inv_variance[0])

    def compute_scratch(pairs):
        return [
            VMEM((count, rows, cols), residual.dtype),
            VMEM((count, rows, cols), f32),
            VMEM((4 * rows, comps * cols), jnp.bfloat16),
            SMEM((epochs,), jnp.int32),
            SMEM((epochs * capacity,), jnp.int32),
            SMEM((epochs * capacity,), jnp.int32),
            SMEM((3, pairs + 1), jnp.int32),
            pltpu.SemaphoreType.DMA((2,)),
        ]

    params = pltpu.CompilerParams(vmem_limit_bytes=24 * MIB)
    band_shapes = [
        jax.ShapeDtypeStruct((comps * cols, 2 * cols), jnp.bfloat16),
        jax.ShapeDtypeStruct((comps * rows, 4 * rows), jnp.bfloat16),
    ]
    pairs = epochs * capacity
    head_jobs, tail_jobs = chunks[:1], chunks[1:]
    made = pl.pallas_call(
        functools.partial(resample_kernel, cfg, True, head_jobs, False),
        out_shape=[slab(size) for _, size in head_jobs for _ in range(n)] + band_shapes,
        in_specs=[smem] * 6 + [hbm] * 2 + [vmem],
        out_specs=[vmem] * (n + 2),
        scratch_shapes=compute_scratch(pairs),
        compiler_params=params,
        name="resample_head",
    )(*scalars, *blocks, psf_taps)
    slabs = [list(made[:n])]
    bands = made[n:]
    made = pl.pallas_call(
        functools.partial(resample_kernel, cfg, False, tail_jobs, True),
        out_shape=[slab(size) for _, size in tail_jobs for _ in range(n)] + [slab(capacity)],
        in_specs=[smem] * 6 + [hbm] * 2 + [vmem] * 2,
        out_specs=[vmem] * (n * len(tail_jobs) + 1),
        scratch_shapes=compute_scratch(pairs),
        compiler_params=params,
        name="resample_tail",
    )(*scalars, *blocks, *bands)
    for k in range(len(tail_jobs)):
        slabs.append(list(made[k * n : (k + 1) * n]))
    own = made[-1]

    def turn(x, d):
        return lax.ppermute(x, "epoch", [(i, (i + d) % epochs) for i in range(epochs)])

    def beside(x, d):
        route = [(i, i + d) for i in range(tiles) if 0 <= i + d < tiles]
        return lax.ppermute(x, "tile", route)

    sends = [
        (capacity if k == 0 else 0) + n * size for k, (_, size) in enumerate(chunks)
    ]
    arrived = []
    waves = []
    total = table = state = None
    for k in range(len(chunks)):
        arrived.append([turn(slabs[k][d - 1], d) for d in range(1, epochs)])
        flat = [x for group in arrived for x in group]
        state_shape = jax.ShapeDtypeStruct((2,), jnp.int32)
        out_shape = [
            jax.ShapeDtypeStruct((cells, rows, cols), f32),
            slab(sends[k]),
            slab(sends[k]),
        ]
        out_specs = [vmem] * 3
        if k == 0:
            out_shape.append(jax.ShapeDtypeStruct((epochs * capacity,), jnp.int32))
            out_specs.append(smem)
            carried, carried_specs = (), []
            scratch = [SMEM((1, LANES), f32)] * epochs + [pltpu.SemaphoreType.DMA((epochs,))]
        else:
            carried, carried_specs = (table, state, total), [smem, smem, vmem]
            scratch = []
        out_shape.append(state_shape)
        out_specs.append(smem)
        result = pl.pallas_call(
            functools.partial(collect_kernel, cfg, chunks, k, sends),
            out_shape=out_shape,
            in_specs=carried_specs + [vmem] * (1 + len(flat)),
            out_specs=out_specs,
            scratch_shapes=scratch,
            compiler_params=params,
            name=f"collect_{k}",
        )(*carried, own, *flat)
        total, state = result[0], result[-1]
        if k == 0:
            table = result[3]
        waves += [beside(result[1], 1), beside(result[2], -1)]
    out = pl.pallas_call(
        functools.partial(finish_kernel, rows),
        out_shape=jax.ShapeDtypeStruct((cells, rows, cols), f32),
        in_specs=[vmem] * (1 + len(waves)),
        out_specs=vmem,
        scratch_shapes=[SMEM((1, LANES), f32)] * len(waves)
        + [pltpu.SemaphoreType.DMA((len(waves),))],
        compiler_params=params,
        name="finish",
    )(total, *waves)
    return out.reshape(1, BANDS, per_dev, rows, cols)


def solution(mesh):
    in_specs = (
        P("tile", "epoch", None, None),
        P("tile", "epoch", None, None),
        P("tile", "epoch", None),
        P(),
        P("tile", "epoch", None),
        P("tile", "epoch"),
        P("tile", "epoch"),
        P("tile", "epoch"),
        P("tile", "epoch"),
    )
    out_specs = P("tile", None, "epoch", None, None)
    body = functools.partial(on_device, mesh.shape["tile"], mesh.shape["epoch"])
    return jax.shard_map(
        body, mesh=mesh, in_specs=in_specs, out_specs=out_specs, check_vma=False
    )
```

```python
import functools

import jax
import jax.numpy as jnp
from jax import lax
from jax.experimental import pallas as pl
from jax.experimental.pallas import tpu as pltpu
from jax.sharding import PartitionSpec as P


BANDS = 6
PATCHES = 32
HEAD = 8
LANES = 128


SMEM = pltpu.SMEM
VMEM = pltpu.VMEM
MIB = 1 << 20


def halves(x):
    high = x.astype(jnp.bfloat16)
    low = (x - high.astype(jnp.float32)).astype(jnp.bfloat16)
    return high, low


def plan_chunks(capacity):
    if capacity >= 16:
        sizes = (capacity // 4, capacity // 2, capacity - capacity // 4 - capacity // 2)
    else:
        sizes = (capacity // 2, capacity - capacity // 2)
    starts = [sum(sizes[:k]) for k in range(len(sizes))]
    return list(zip(starts, sizes))


def head_lanes():
    return lax.broadcasted_iota(jnp.int32, (HEAD, LANES), 1)


def build_bands(taps_ref, cols_ref, rows_ref):
    comps, _, taps = taps_ref.shape
    cols = cols_ref.shape[1] // 2
    rows = rows_ref.shape[1] // 4
    half = (taps - 1) // 2
    tap = lax.broadcasted_iota(jnp.int32, (taps, LANES), 0)
    lane = lax.broadcasted_iota(jnp.int32, (taps, LANES), 1)
    place_col = (lax.rem(lane + tap - half + cols, cols) == 0).astype(jnp.float32)
    place_row = (lax.rem(lane - tap + half + 2 * rows, rows) == 0).astype(jnp.float32)
    base_col = jnp.dot(
        taps_ref[:, 0, :], place_col, precision=lax.Precision.HIGHEST,
        preferred_element_type=jnp.float32,
    )
    base_row = jnp.dot(
        taps_ref[:, 1, :], place_row, precision=lax.Precision.HIGHEST,
        preferred_element_type=jnp.float32,
    )
    up = lax.broadcasted_iota(jnp.int32, (cols, LANES), 0)
    across = lax.broadcasted_iota(jnp.int32, (cols, LANES), 1)
    near_col = jnp.abs(across - up) <= half
    up_row = lax.broadcasted_iota(jnp.int32, (rows, LANES), 0)
    across_row = lax.rem(lax.broadcasted_iota(jnp.int32, (rows, LANES), 1), rows)
    near_row = jnp.abs(across_row - up_row) <= half
    for c in range(comps):
        wide = jnp.broadcast_to(base_col[c : c + 1, :], (cols, LANES))
        wide = pltpu.roll(wide, 0, 1, stride=1, stride_axis=0)
        high, low = halves(jnp.where(near_col, wide, 0.0))
        cols_ref[c * cols : (c + 1) * cols, :] = jnp.concatenate([high, low], axis=1)
        wide = jnp.broadcast_to(base_row[c : c + 1, :], (rows, LANES))
        wide = pltpu.roll(wide, 0, 1, stride=1, stride_axis=0)
        high, low = halves(jnp.where(near_row, wide, 0.0))
        rows_ref[c * rows : (c + 1) * rows, :] = jnp.concatenate([high, low], axis=1)


def resample_kernel(cfg, first, jobs, with_self, *refs):
    epochs, capacity, per_dev, tiles, count, rows, cols = cfg
    cells = BANDS * per_dev
    n_out = len(jobs) * (epochs - 1) + (1 if with_self else 0)
    places_hbm = refs[:5]
    coeff_hbm, res_hbm, inv_hbm = refs[5:8]
    if first:
        taps_hbm = refs[8]
        rest = refs[9:]
        outs, (cols_ref, rows_ref) = rest[:n_out], rest[n_out : n_out + 2]
        rest = rest[n_out + 2 :]
    else:
        cols_ref, rows_ref = refs[8:10]
        rest = refs[10:]
        outs = rest[:n_out]
        rest = rest[n_out:]
    places = rest[:5]
    owner_ref, slot_ref, band_ref, offset_ref, shift_ref = places
    coeff_ref, res_ref, inv_ref, taps_ref = rest[5:9]
    spread_ref, front_ref, back_ref, block_ref, label_ref, todo_ref, sems = rest[9:]

    pieces = [*zip(places_hbm, places), (coeff_hbm, coeff_ref)]
    if first:
        pieces.append((taps_hbm, taps_ref))
    pieces += [(res_hbm, res_ref), (inv_hbm, inv_ref)]
    fetches = [
        pltpu.make_async_copy(src, dst, sems.at[i]) for i, (src, dst) in enumerate(pieces)
    ]
    for fetch in fetches:
        fetch.start()

    me = lax.axis_index("epoch")
    tile = lax.axis_index("tile")
    for e in range(epochs):
        front_ref[e] = e * capacity
        back_ref[e] = (e + 1) * capacity - 1
    for i in range(epochs * capacity):
        label_ref[i] = 0
        block_ref[i] = 0
    if first:
        fetches[6].wait()
        build_bands(taps_ref, cols_ref, rows_ref)
    for fetch in fetches[:5]:
        fetch.wait()

    def place(b, carry):
        off = offset_ref[b]
        target = tile + off - 1

        @pl.when((target >= 0) & (target < tiles))
        def _():
            o = owner_ref[b]
            front = front_ref[o]
            back = back_ref[o]
            stays = (off == 1).astype(jnp.int32)
            at = jnp.where(off == 1, back, front)
            front_ref[o] = front + 1 - stays
            back_ref[o] = back - stays
            block_ref[at] = b
            label_ref[at] = off * cells + band_ref[b] * per_dev + slot_ref[b] + 1

        return carry

    lax.fori_loop(0, count, place, 0)

    total = jnp.int32(0)
    parts = [(d, start, size) for start, size in jobs for d in range(1, epochs)]
    if with_self:
        parts.append((0, 0, capacity))
    for out_at, (d, start, size) in enumerate(parts):
        o = lax.rem(me + d, epochs)
        for s in range(0, size, 2):
            at = o * capacity + start + s
            todo_ref[0, total] = at
            todo_ref[1, total] = out_at
            todo_ref[2, total] = s
            some = label_ref[at]
            if s + 1 < size:
                some = some + label_ref[at + 1]
            total = total + (some > 0).astype(jnp.int32)

    lane = head_lanes()
    for out_at, (d, start, size) in enumerate(parts):
        if start == 0:
            o = lax.rem(me + d, epochs)
            head = jnp.zeros((HEAD, LANES), jnp.float32)
            for j in range(capacity):
                head = jnp.where(
                    lane == j, label_ref[o * capacity + j].astype(jnp.float32), head
                )
            outs[out_at][size * rows : size * rows + HEAD, :] = head

    fetches[5].wait()
    fetches[-2].wait()
    fetches[-1].wait()
    comps = cols_ref.shape[0] // cols

    def work(i, carry):
        at = todo_ref[0, i]
        out_at = todo_ref[1, i]
        s = todo_ref[2, i]
        blocks = [block_ref[at], block_ref[jnp.minimum(at + 1, epochs * capacity - 1)]]
        sides = []
        for b in blocks:
            high, low = halves(inv_ref[b] * res_ref[b].astype(jnp.float32))
            sides.append(jnp.concatenate([high, low, high, low], axis=0))
        down = jnp.dot(
            rows_ref[...], jnp.concatenate(sides, axis=1), preferred_element_type=jnp.float32
        )
        for c in range(comps):
            for g in range(2):
                part = down[c * rows : (c + 1) * rows, g * cols : (g + 1) * cols]
                high, low = halves(part * coeff_ref[c, blocks[g]])
                spread_ref[g * rows : (g + 1) * rows, c * cols : (c + 1) * cols] = high
                spread_ref[(2 + g) * rows : (3 + g) * rows, c * cols : (c + 1) * cols] = low
        both = jnp.dot(spread_ref[...], cols_ref[...], preferred_element_type=jnp.float32)
        lanes = lax.broadcasted_iota(jnp.int32, (rows, cols), 1)
        for g in range(2):
            high = both[g * rows : (g + 1) * rows]
            low = both[(2 + g) * rows : (3 + g) * rows]
            image = high[:, :cols] + (high[:, cols:] + low[:, :cols])
            shift = shift_ref[blocks[g]]
            image = jnp.where(lanes >= shift, pltpu.roll(image, shift, 1), 0.0)
            for k, (d, start, size) in enumerate(parts):
                last = size % 2 == 1

                @pl.when((out_at == k) & ((s + g < size) if last else True))
                def _():
                    outs[k][pl.ds(pl.multiple_of((s + g) * rows, rows), rows), :] = image

        return carry

    lax.fori_loop(0, total, work, 0)


def read_heads(sources, head_refs, sems):
    copies = [
        pltpu.make_async_copy(src.at[pl.ds(src.shape[0] - HEAD, 1)], dst, sems.at[i])
        for i, (src, dst) in enumerate(zip(sources, head_refs))
    ]
    for copy in copies:
        copy.start()
    for copy in copies:
        copy.wait()


PITCH = 1024


class Queues:
    def __init__(self, cfg, chunks, sends):
        epochs, capacity = cfg[:2]
        self.sources = [(0, 0, 0, capacity)] + [
            (k, d, start, size) for k, (start, size) in enumerate(chunks) for d in range(1, epochs)
        ]
        self.slots = epochs * capacity
        self.waves = len(chunks)
        self.ends = 3 * self.slots + 1
        self.limits = self.ends + 3 * len(self.sources)
        self.size = self.limits + 2 * 2 * self.waves
        self.sends = sends

    def entry(self, which, i):
        return which * self.slots + i

    def end(self, which, source):
        return self.ends + which * len(self.sources) + source

    def limit(self, side, wave):
        return self.limits + 2 * (side * self.waves + wave)

    def fill(self, table, labels, cells):
        counts = (jnp.int32(0),) * 3
        for at, (k, d, start, size) in enumerate(self.sources):

            def step(j, counts, d=d, start=start):
                label = labels(d, start + j)
                kind = (label > cells).astype(jnp.int32) + (label > 2 * cells).astype(jnp.int32)
                some = label > 0
                n = jnp.where(kind == 0, counts[0], jnp.where(kind == 1, counts[1], counts[2]))
                place = jnp.where(some, kind * self.slots + n, 3 * self.slots)
                table[place] = j * PITCH + label - 1 - kind * cells
                return tuple(
                    c + (some & (kind == w)).astype(jnp.int32) for w, c in enumerate(counts)
                )

            counts = lax.fori_loop(0, size, step, counts)
            for w in range(3):
                table[self.end(w, at)] = counts[w]
        for side, which in enumerate((0, 2)):
            sent = jnp.int32(0)
            for k in range(self.waves):
                last = max(i for i, source in enumerate(self.sources) if source[0] == k)
                table[self.limit(side, k)] = sent
                sent = jnp.minimum(table[self.end(which, last)], sent + self.sends[k])
                table[self.limit(side, k) + 1] = sent


def collect_kernel(cfg, queues, k, *refs):
    epochs, _, per_dev, _, _, rows, _ = cfg
    cells = BANDS * per_dev
    known = [i for i, source in enumerate(queues.sources) if source[0] <= k]
    if k == 0:
        sources, rest = refs[: len(known)], refs[len(known) :]
        prev_ref, next_ref, table = rest[:3]
        head_refs, sems = rest[3 : 3 + epochs], rest[3 + epochs]
        read_heads(sources, head_refs, sems)
        queues.fill(table, lambda d, j: head_refs[d][0, j].astype(jnp.int32), cells)
    else:
        table, sources, rest = refs[0], refs[1 : 1 + len(known)], refs[1 + len(known) :]
        prev_ref, next_ref = rest[:2]
    lane = head_lanes()
    cap = queues.sends[k]
    for side, (which, dst) in enumerate(((0, prev_ref), (2, next_ref))):
        first = table[queues.limit(side, k)]
        last = table[queues.limit(side, k) + 1]
        for i, src in zip(known, sources):
            low = table[queues.end(which, i - 1)] if i else 0
            high = table[queues.end(which, i)]

            def step(r, carry, which=which, src=src, dst=dst, first=first):
                j = table[queues.entry(which, r)] // PITCH
                dst[pl.ds(pl.multiple_of((r - first) * rows, rows), rows), :] = src[
                    pl.ds(pl.multiple_of(j * rows, rows), rows), :
                ]
                return carry

            lax.fori_loop(jnp.maximum(low, first), jnp.minimum(high, last), step, 0)

        def mark(r, head, which=which, first=first):
            cell = table[queues.entry(which, r)] % PITCH
            return jnp.where(lane == r - first, cell.astype(jnp.float32), head)

        amount = jnp.where(lane == LANES - 1, (last - first).astype(jnp.float32), 0.0)
        dst[cap * rows : cap * rows + HEAD, :] = lax.fori_loop(first, last, mark, amount)


def add_waves(total_ref, waves, head_refs, rows):
    for src, head in zip(waves, head_refs):

        def step(j, carry, src=src, head=head):
            cell = head[0, j].astype(jnp.int32)
            block = pl.ds(pl.multiple_of(j * rows, rows), rows)
            total_ref[cell] = total_ref[cell] + src[block, :]
            return carry

        lax.fori_loop(0, head[0, LANES - 1].astype(jnp.int32), step, 0)


def settle_kernel(cfg, queues, *refs):
    rows = cfg[5]
    n = len(queues.sources)
    table, sources, rest = refs[0], refs[1 : 1 + n], refs[1 + n :]
    waves = (len(rest) - 2) // 2
    early, total_ref, head_refs, sems = rest[:waves], rest[waves], rest[waves + 1 : -1], rest[-1]
    total_ref[...] = jnp.zeros_like(total_ref)
    for i, src in enumerate(sources):

        def step(r, carry, src=src):
            entry = table[queues.entry(1, r)]
            cell = entry % PITCH
            block = pl.ds(pl.multiple_of((entry // PITCH) * rows, rows), rows)
            total_ref[cell] = total_ref[cell] + src[block, :]
            return carry

        low = table[queues.end(1, i - 1)] if i else 0
        lax.fori_loop(low, table[queues.end(1, i)], step, 0)
    read_heads(early, head_refs, sems)
    add_waves(total_ref, early, head_refs, rows)


def finish_kernel(rows, *refs):
    waves = (len(refs) - 3) // 2
    total_ref, sources, out_ref = refs[0], refs[1 : 1 + waves], refs[1 + waves]
    head_refs, sems = refs[2 + waves : -1], refs[-1]
    out_ref[...] = total_ref[...]
    read_heads(sources, head_refs, sems)
    add_waves(out_ref, sources, head_refs, rows)


def on_device(
    tiles,
    epochs,
    residual,
    inv_variance,
    psf_coeff,
    psf_taps,
    patch_owner,
    patch_slot,
    band_id,
    tile_offset,
    col_shift,
):
    count, rows, cols = residual.shape[1:]
    comps = psf_taps.shape[0]
    capacity = max(2, min(count // 2, 64 // epochs))
    per_dev = PATCHES // epochs
    cells = BANDS * per_dev
    cfg = (epochs, capacity, per_dev, tiles, count, rows, cols)
    chunks = plan_chunks(capacity)
    n = epochs - 1
    f32 = jnp.float32
    smem = pl.BlockSpec(memory_space=SMEM)
    vmem = pl.BlockSpec(memory_space=VMEM)
    hbm = pl.BlockSpec(memory_space=pltpu.HBM)

    def slab(slots):
        return jax.ShapeDtypeStruct((slots * rows + HEAD, cols), f32)

    inputs = (
        patch_owner.reshape(count),
        patch_slot.reshape(count),
        band_id.reshape(count),
        tile_offset.reshape(count),
        col_shift.reshape(count),
        psf_coeff[0].T,
        residual[0],
        inv_variance[0],
        psf_taps,
    )
    inputs = tuple(pltpu.with_memory_space_constraint(x, pltpu.HBM) for x in inputs)
    pairs = epochs * capacity
    scratch = [
        *[SMEM((count,), jnp.int32)] * 5,
        SMEM((comps, count), f32),
        VMEM((count, rows, cols), residual.dtype),
        VMEM((count, rows, cols), f32),
        VMEM(psf_taps.shape, f32),
        VMEM((4 * rows, comps * cols), jnp.bfloat16),
        SMEM((epochs,), jnp.int32),
        SMEM((epochs,), jnp.int32),
        SMEM((epochs * capacity,), jnp.int32),
        SMEM((epochs * capacity,), jnp.int32),
        SMEM((3, pairs + 1), jnp.int32),
        pltpu.SemaphoreType.DMA((9,)),
    ]

    params = pltpu.CompilerParams(vmem_limit_bytes=24 * MIB)
    band_shapes = [
        jax.ShapeDtypeStruct((comps * cols, 2 * cols), jnp.bfloat16),
        jax.ShapeDtypeStruct((comps * rows, 4 * rows), jnp.bfloat16),
    ]
    head_jobs, tail_jobs = chunks[:1], chunks[1:]
    made = pl.pallas_call(
        functools.partial(resample_kernel, cfg, True, head_jobs, False),
        out_shape=[slab(size) for _, size in head_jobs for _ in range(n)] + band_shapes,
        in_specs=[hbm] * 9,
        out_specs=[vmem] * (n + 2),
        scratch_shapes=scratch,
        compiler_params=params,
        name="resample_head",
    )(*inputs)
    slabs = [list(made[:n])]
    bands = made[n:]
    made = pl.pallas_call(
        functools.partial(resample_kernel, cfg, False, tail_jobs, True),
        out_shape=[slab(size) for _, size in tail_jobs for _ in range(n)] + [slab(capacity)],
        in_specs=[hbm] * 8 + [vmem] * 2,
        out_specs=[vmem] * (n * len(tail_jobs) + 1),
        scratch_shapes=scratch,
        compiler_params=params,
        name="resample_tail",
    )(*inputs[:-1], *bands)
    for k in range(len(tail_jobs)):
        slabs.append(list(made[k * n : (k + 1) * n]))
    own = made[-1]

    def turn(x, d):
        return lax.ppermute(x, "epoch", [(i, (i + d) % epochs) for i in range(epochs)])

    def beside(x, d):
        route = [(i, i + d) for i in range(tiles) if 0 <= i + d < tiles]
        return lax.ppermute(x, "tile", route)

    sends = [
        (capacity if k == 0 else 0) + n * size for k, (_, size) in enumerate(chunks)
    ]
    queues = Queues(cfg, chunks, sends)
    sources = [own]
    waves = []
    table = None
    for k in range(len(chunks)):
        sources += [turn(slabs[k][d - 1], d) for d in range(1, epochs)]
        out_shape = [slab(sends[k])] * 2
        out_specs = [vmem] * 2
        extra = []
        if k == 0:
            out_shape.append(jax.ShapeDtypeStruct((queues.size,), jnp.int32))
            out_specs.append(smem)
            extra = [SMEM((1, LANES), f32)] * epochs + [pltpu.SemaphoreType.DMA((epochs,))]
        result = pl.pallas_call(
            functools.partial(collect_kernel, cfg, queues, k),
            out_shape=out_shape,
            in_specs=([smem] if k else []) + [vmem] * len(sources),
            out_specs=out_specs,
            scratch_shapes=extra,
            compiler_params=params,
        )(*([table] if k else []), *sources)
        if k == 0:
            table = result[2]
        waves.append([beside(result[0], -1), beside(result[1], 1)])
    early = [x for wave in waves[:-1] for x in wave]
    late = waves[-1]
    total_shape = jax.ShapeDtypeStruct((cells, rows, cols), f32)

    def heads(arrays):
        return [SMEM((1, LANES), f32)] * len(arrays) + [
            pltpu.SemaphoreType.DMA((len(arrays),))
        ]

    total = pl.pallas_call(
        functools.partial(settle_kernel, cfg, queues),
        out_shape=total_shape,
        in_specs=[smem] + [vmem] * (len(sources) + len(early)),
        out_specs=vmem,
        scratch_shapes=heads(early),
        compiler_params=params,
        name="settle",
    )(table, *sources, *early)
    out = pl.pallas_call(
        functools.partial(finish_kernel, rows),
        out_shape=total_shape,
        in_specs=[vmem] * (1 + len(late)),
        out_specs=vmem,
        scratch_shapes=heads(late),
        compiler_params=params,
        name="finish",
    )(total, *late)
    return out.reshape(1, BANDS, per_dev, rows, cols)


def solution(mesh):
    in_specs = (
        P("tile", "epoch", None, None),
        P("tile", "epoch", None, None),
        P("tile", "epoch", None),
        P(),
        P("tile", "epoch", None),
        P("tile", "epoch"),
        P("tile", "epoch"),
        P("tile", "epoch"),
        P("tile", "epoch"),
    )
    out_specs = P("tile", None, "epoch", None, None)
    epochs = mesh.shape["epoch"]
    device = functools.partial(on_device, mesh.shape["tile"], epochs)

    return jax.shard_map(device, mesh=mesh, in_specs=in_specs, out_specs=out_specs, check_vma=False)
```

```python
import functools

import jax
import jax.numpy as jnp
from jax import lax
from jax.experimental import pallas as pl
from jax.experimental.pallas import tpu as pltpu
from jax.sharding import PartitionSpec as P


BANDS = 6
PATCHES = 32
HEAD = 8
LANES = 128


SMEM = pltpu.SMEM
VMEM = pltpu.VMEM
MIB = 1 << 20


def halves(x):
    high = x.astype(jnp.bfloat16)
    low = (x - high.astype(jnp.float32)).astype(jnp.bfloat16)
    return high, low


def plan_chunks(capacity):
    if capacity >= 16:
        sizes = (capacity // 4, capacity // 2, capacity - capacity // 4 - capacity // 2)
    else:
        sizes = (capacity // 2, capacity - capacity // 2)
    starts = [sum(sizes[:k]) for k in range(len(sizes))]
    return list(zip(starts, sizes))


def head_lanes():
    return lax.broadcasted_iota(jnp.int32, (HEAD, LANES), 1)


def build_bands(taps_ref, cols_ref, rows_ref):
    comps, _, taps = taps_ref.shape
    cols = cols_ref.shape[1] // 2
    rows = rows_ref.shape[1] // 4
    half = (taps - 1) // 2
    tap = lax.broadcasted_iota(jnp.int32, (taps, LANES), 0)
    lane = lax.broadcasted_iota(jnp.int32, (taps, LANES), 1)
    place_col = (lax.rem(lane + tap - half + cols, cols) == 0).astype(jnp.float32)
    place_row = (lax.rem(lane - tap + half + 2 * rows, rows) == 0).astype(jnp.float32)
    base_col = jnp.dot(
        taps_ref[:, 0, :], place_col, precision=lax.Precision.HIGHEST,
        preferred_element_type=jnp.float32,
    )
    base_row = jnp.dot(
        taps_ref[:, 1, :], place_row, precision=lax.Precision.HIGHEST,
        preferred_element_type=jnp.float32,
    )
    up = lax.broadcasted_iota(jnp.int32, (cols, LANES), 0)
    across = lax.broadcasted_iota(jnp.int32, (cols, LANES), 1)
    near_col = jnp.abs(across - up) <= half
    up_row = lax.broadcasted_iota(jnp.int32, (rows, LANES), 0)
    across_row = lax.rem(lax.broadcasted_iota(jnp.int32, (rows, LANES), 1), rows)
    near_row = jnp.abs(across_row - up_row) <= half
    for c in range(comps):
        wide = jnp.broadcast_to(base_col[c : c + 1, :], (cols, LANES))
        wide = pltpu.roll(wide, 0, 1, stride=1, stride_axis=0)
        high, low = halves(jnp.where(near_col, wide, 0.0))
        cols_ref[c * cols : (c + 1) * cols, :] = jnp.concatenate([high, low], axis=1)
        wide = jnp.broadcast_to(base_row[c : c + 1, :], (rows, LANES))
        wide = pltpu.roll(wide, 0, 1, stride=1, stride_axis=0)
        high, low = halves(jnp.where(near_row, wide, 0.0))
        rows_ref[c * rows : (c + 1) * rows, :] = jnp.concatenate([high, low], axis=1)


def fill_slots(cfg, places, block_ref, label_ref, front_ref, back_ref):
    epochs, capacity, per_dev, tiles, count, _, _ = cfg
    cells = BANDS * per_dev
    owner_ref, slot_ref, band_ref, offset_ref = places
    tile = lax.axis_index("tile")
    for e in range(epochs):
        front_ref[e] = e * capacity
        back_ref[e] = (e + 1) * capacity - 1

    def place(b, carry):
        off = offset_ref[b]
        target = tile + off - 1

        @pl.when((target >= 0) & (target < tiles))
        def _():
            o = owner_ref[b]
            front = front_ref[o]
            back = back_ref[o]
            stays = (off == 1).astype(jnp.int32)
            at = jnp.where(off == 1, back, front)
            front_ref[o] = front + 1 - stays
            back_ref[o] = back - stays
            block_ref[at] = b
            label_ref[at] = off * cells + band_ref[b] * per_dev + slot_ref[b] + 1

        return carry

    lax.fori_loop(0, count, place, 0)


def resample_kernel(cfg, first, jobs, with_self, *refs):
    epochs, capacity, _, _, _, rows, cols = cfg
    slots = epochs * capacity
    n_out = len(jobs) * (epochs - 1) + (1 if with_self else 0)
    if first:
        small_hbm, large_hbm, rest = refs[:6], refs[6:9], refs[9:]
        outs, rest = rest[:n_out], rest[n_out:]
        cols_ref, rows_ref, res_ref, inv_ref, block_ref, label_ref = rest[:6]
        shift_ref, coeff_ref, *places, taps_ref, front_ref, back_ref = rest[6:15]
        small = [*places, shift_ref, coeff_ref]
        rest = rest[15:]
        pieces = [
            *zip(small_hbm, small),
            *zip(large_hbm, (taps_ref, res_ref, inv_ref)),
        ]
    else:
        block_ref, label_ref, shift_ref, coeff_ref = refs[:4]
        cols_ref, rows_ref, res_ref, inv_ref = refs[4:8]
        outs, rest = refs[8 : 8 + n_out], refs[8 + n_out :]
        pieces = []
    spread_refs, todo_ref, sems = rest[:2], rest[2], rest[3]
    fetches = [
        pltpu.make_async_copy(src, dst, sems.at[i]) for i, (src, dst) in enumerate(pieces)
    ]
    for fetch in fetches:
        fetch.start()

    if first:
        for i in range(slots):
            label_ref[i] = 0
            block_ref[i] = 0
        fetches[6].wait()
        build_bands(taps_ref, cols_ref, rows_ref)
        for fetch in fetches[:4]:
            fetch.wait()
        fill_slots(cfg, places, block_ref, label_ref, front_ref, back_ref)

    me = lax.axis_index("epoch")
    total = jnp.int32(0)
    parts = [(d, start, size) for start, size in jobs for d in range(1, epochs)]
    if with_self:
        parts.append((0, 0, capacity))
    for k, (d, start, size) in enumerate(parts):
        o = lax.rem(me + d, epochs)
        for s in range(size):
            at = o * capacity + start + s
            todo_ref[0, total] = block_ref[at]
            todo_ref[1, total] = k * slots + s
            total = total + (label_ref[at] > 0).astype(jnp.int32)
    for i in range(3):
        todo_ref[0, total + i] = 0
        todo_ref[1, total + i] = len(parts) * slots

    lane = head_lanes()
    if any(start == 0 for _, start, _ in parts):
        head = jnp.zeros((HEAD, LANES), jnp.float32)
        for j in range(slots):
            head = jnp.where(lane == j, label_ref[j].astype(jnp.float32), head)
        for k, (d, start, size) in enumerate(parts):
            if start == 0:
                outs[k][size * rows : size * rows + HEAD, :] = head

    for fetch in fetches[4:6] + fetches[7:]:
        fetch.wait()
    comps = cols_ref.shape[0] // cols
    lanes = lax.broadcasted_iota(jnp.int32, (rows, cols), 1)

    def work(base, twos):
        jobs_here = [(todo_ref[0, base + g], todo_ref[1, base + g]) for g in range(2 * twos)]
        for t in range(twos):
            blocks = [b for b, _ in jobs_here[2 * t : 2 * t + 2]]
            spread_ref = spread_refs[t]
            sides = []
            for b in blocks:
                high, low = halves(inv_ref[b] * res_ref[b].astype(jnp.float32))
                sides.append(jnp.concatenate([high, low, high, low], axis=0))
            down = jnp.dot(
                rows_ref[...],
                jnp.concatenate(sides, axis=1),
                preferred_element_type=jnp.float32,
            )
            for c in range(comps):
                for g in range(2):
                    part = down[c * rows : (c + 1) * rows, g * cols : (g + 1) * cols]
                    high, low = halves(part * coeff_ref[c, blocks[g]])
                    at = slice(c * cols, (c + 1) * cols)
                    spread_ref[g * rows : (g + 1) * rows, at] = high
                    spread_ref[(2 + g) * rows : (3 + g) * rows, at] = low
        images = []
        for t in range(twos):
            both = jnp.dot(
                spread_refs[t][...], cols_ref[...], preferred_element_type=jnp.float32
            )
            for g in range(2):
                b, where = jobs_here[2 * t + g]
                high = both[g * rows : (g + 1) * rows]
                low = both[(2 + g) * rows : (3 + g) * rows]
                image = high[:, :cols] + (high[:, cols:] + low[:, :cols])
                shift = shift_ref[b]
                images.append(jnp.where(lanes >= shift, pltpu.roll(image, shift, 1), 0.0))
        for (_, where), image in zip(jobs_here, images):
            for k in range(len(parts)):

                @pl.when((where >= k * slots) & (where < (k + 1) * slots))
                def _():
                    s = pl.multiple_of((where - k * slots) * rows, rows)
                    outs[k][pl.ds(s, rows), :] = image

    quads = (total + 1) // 4

    def quad(i, carry):
        work(4 * i, 2)
        return carry

    lax.fori_loop(0, quads, quad, 0)

    @pl.when(total > 4 * quads)
    def _():
        work(4 * quads, 1)


def read_heads(sources, head_refs, sems):
    copies = [
        pltpu.make_async_copy(src.at[pl.ds(src.shape[0] - HEAD, 1)], dst, sems.at[i])
        for i, (src, dst) in enumerate(zip(sources, head_refs))
    ]
    for copy in copies:
        copy.start()
    for copy in copies:
        copy.wait()


PITCH = 1024


class Queues:
    def __init__(self, cfg, chunks, sends):
        epochs, capacity = cfg[:2]
        self.sources = [(0, 0, 0, capacity)] + [
            (k, d, start, size) for k, (start, size) in enumerate(chunks) for d in range(1, epochs)
        ]
        self.slots = epochs * capacity
        self.waves = len(chunks)
        self.ends = 3 * self.slots + 1
        self.limits = self.ends + 3 * len(self.sources)
        self.size = self.limits + 2 * 2 * self.waves
        self.sends = sends
        self.capacity = capacity

    def entry(self, which, i):
        return which * self.slots + i

    def end(self, which, source):
        return self.ends + which * len(self.sources) + source

    def limit(self, side, wave):
        return self.limits + 2 * (side * self.waves + wave)

    def fill(self, table, labels, cells):
        counts = (jnp.int32(0),) * 3
        for at, (k, d, start, size) in enumerate(self.sources):

            def step(j, counts, d=d, start=start):
                label = labels(d, start + j)
                kind = (label > cells).astype(jnp.int32) + (label > 2 * cells).astype(jnp.int32)
                some = label > 0
                n = jnp.where(kind == 0, counts[0], jnp.where(kind == 1, counts[1], counts[2]))
                place = jnp.where(some, kind * self.slots + n, 3 * self.slots)
                table[place] = j * PITCH + label - 1 - kind * cells
                return tuple(
                    c + (some & (kind == w)).astype(jnp.int32) for w, c in enumerate(counts)
                )

            counts = lax.fori_loop(0, size, step, counts)
            for w in range(3):
                table[self.end(w, at)] = counts[w]
        for side, which in enumerate((0, 2)):
            sent = jnp.int32(0)
            for k in range(self.waves):
                last = max(i for i, source in enumerate(self.sources) if source[0] == k)
                table[self.limit(side, k)] = sent
                sent = jnp.minimum(table[self.end(which, last)], sent + self.sends[k])
                table[self.limit(side, k) + 1] = sent


    def overflow(self, heads, cells, ends):
        slot = lax.broadcasted_iota(jnp.int32, (LANES, LANES), 0)
        epoch = lax.broadcasted_iota(jnp.int32, (LANES, LANES), 1)
        mine = lax.div(slot, self.capacity) == epoch
        over = jnp.zeros((HEAD, LANES), jnp.float32)
        for low, high in ((0, cells), (2 * cells, 3 * cells)):
            amount = jnp.zeros((HEAD, LANES), jnp.float32)
            for head in heads:
                amount = amount + jnp.where((head > low) & (head <= high), 1.0, 0.0)
            sent = jnp.zeros((HEAD, LANES), jnp.float32)
            for end, cap in zip(ends, self.sends):
                here = jnp.where(mine & (lax.rem(slot, self.capacity) < end), 1.0, 0.0)
                have = jnp.dot(
                    amount.astype(jnp.bfloat16),
                    here.astype(jnp.bfloat16),
                    preferred_element_type=jnp.float32,
                )
                sent = jnp.minimum(have, sent + cap)
            over = jnp.maximum(over, jnp.where(have > sent, 1.0, 0.0))
        return over


def collect_kernel(cfg, queues, k, ends, *refs):
    epochs, capacity, per_dev, _, _, rows, _ = cfg
    cells = BANDS * per_dev
    known = [i for i, source in enumerate(queues.sources) if source[0] <= k]
    if k == 0:
        sources, rest = refs[: len(known)], refs[len(known) :]
        prev_ref, next_ref, table, over_ref = rest[:4]
        head_refs, sems = rest[4 : 4 + epochs], rest[4 + epochs]
        read_heads(sources, head_refs, sems)
        mine = lax.axis_index("epoch") * capacity
        queues.fill(table, lambda d, j: head_refs[d][0, mine + j].astype(jnp.int32), cells)
        heads = [src[src.shape[0] - HEAD :, :] for src in sources]
        over = jnp.max(queues.overflow(heads, cells, ends), axis=1, keepdims=True)
        over_ref[...] = jnp.broadcast_to(over, over_ref.shape)
    else:
        table, mine_ref, theirs_ref = refs[:3]
        sources, rest = refs[3 : 3 + len(known)], refs[3 + len(known) :]
        prev_ref, next_ref, over_ref = rest
        over_ref[...] = jnp.maximum(mine_ref[...], theirs_ref[...])
    lane = head_lanes()
    cap = queues.sends[k]
    for side, (which, dst) in enumerate(((0, prev_ref), (2, next_ref))):
        first = table[queues.limit(side, k)]
        last = table[queues.limit(side, k) + 1]
        for i, src in zip(known, sources):
            low = table[queues.end(which, i - 1)] if i else 0
            high = table[queues.end(which, i)]

            def step(r, carry, which=which, src=src, dst=dst, first=first):
                j = table[queues.entry(which, r)] // PITCH
                dst[pl.ds(pl.multiple_of((r - first) * rows, rows), rows), :] = src[
                    pl.ds(pl.multiple_of(j * rows, rows), rows), :
                ]
                return carry

            lax.fori_loop(jnp.maximum(low, first), jnp.minimum(high, last), step, 0)

        def mark(r, head, which=which, first=first):
            cell = table[queues.entry(which, r)] % PITCH
            return jnp.where(lane == r - first, cell.astype(jnp.float32), head)

        amount = jnp.where(lane == LANES - 1, (last - first).astype(jnp.float32), 0.0)
        dst[cap * rows : cap * rows + HEAD, :] = lax.fori_loop(first, last, mark, amount)


def add_waves(total_ref, waves, head_refs, rows):
    for src, head in zip(waves, head_refs):

        def step(j, carry, src=src, head=head):
            cell = head[0, j].astype(jnp.int32)
            block = pl.ds(pl.multiple_of(j * rows, rows), rows)
            total_ref[cell] = total_ref[cell] + src[block, :]
            return carry

        lax.fori_loop(0, head[0, LANES - 1].astype(jnp.int32), step, 0)


def settle_kernel(cfg, queues, *refs):
    rows = cfg[5]
    n = len(queues.sources)
    table, sources, rest = refs[0], refs[1 : 1 + n], refs[1 + n :]
    waves = (len(rest) - 2) // 2
    early, total_ref, head_refs, sems = rest[:waves], rest[waves], rest[waves + 1 : -1], rest[-1]
    total_ref[...] = jnp.zeros_like(total_ref)
    for i, src in enumerate(sources):

        def step(r, carry, src=src):
            entry = table[queues.entry(1, r)]
            cell = entry % PITCH
            block = pl.ds(pl.multiple_of((entry // PITCH) * rows, rows), rows)
            total_ref[cell] = total_ref[cell] + src[block, :]
            return carry

        low = table[queues.end(1, i - 1)] if i else 0
        lax.fori_loop(low, table[queues.end(1, i)], step, 0)
    read_heads(early, head_refs, sems)
    add_waves(total_ref, early, head_refs, rows)


def finish_kernel(rows, *refs):
    total_ref, mine_ref, theirs_ref = refs[:3]
    waves = (len(refs) - 8) // 2
    sources, (out_ref, failed_ref) = refs[3 : 3 + waves], refs[3 + waves : 5 + waves]
    head_refs, (over_ref, said_ref, sems) = refs[5 + waves : -3], refs[-3:]
    over_ref[...] = jnp.maximum(mine_ref[...], theirs_ref[...])
    say = pltpu.make_async_copy(over_ref.at[pl.ds(0, 1)], said_ref, sems.at[waves])
    say.start()
    out_ref[...] = total_ref[...]
    read_heads(sources, head_refs, sems)
    add_waves(out_ref, sources, head_refs, rows)
    say.wait()
    failed_ref[0] = (said_ref[0, 0] > 0.0).astype(jnp.int32)


def run(cfg, sends, args):
    (
        residual, inv_variance, psf_coeff, psf_taps, patch_owner,
        patch_slot, band_id, tile_offset, col_shift,
    ) = args
    epochs, capacity, per_dev, tiles, count, rows, cols = cfg
    comps = psf_taps.shape[0]
    cells = BANDS * per_dev
    chunks = plan_chunks(capacity)
    ends = [start + size for start, size in chunks]
    n = epochs - 1
    full = [(capacity if k == 0 else 0) + n * size for k, (_, size) in enumerate(chunks)]
    checked = any(cap < most for cap, most in zip(sends, full))
    f32 = jnp.float32
    smem = pl.BlockSpec(memory_space=SMEM)
    vmem = pl.BlockSpec(memory_space=VMEM)
    hbm = pl.BlockSpec(memory_space=pltpu.HBM)

    def slab(slots):
        return jax.ShapeDtypeStruct((slots * rows + HEAD, cols), f32)

    inputs = (
        patch_owner.reshape(count),
        patch_slot.reshape(count),
        band_id.reshape(count),
        tile_offset.reshape(count),
        col_shift.reshape(count),
        psf_coeff[0].T,
        psf_taps,
        residual[0],
        inv_variance[0],
    )
    inputs = tuple(pltpu.with_memory_space_constraint(x, pltpu.HBM) for x in inputs)
    slots = epochs * capacity
    common = [
        *[VMEM((4 * rows, comps * cols), jnp.bfloat16)] * 2,
        SMEM((2, slots + 3), jnp.int32),
        pltpu.SemaphoreType.DMA((9,)),
    ]
    params = pltpu.CompilerParams(vmem_limit_bytes=24 * MIB)
    kept = [
        jax.ShapeDtypeStruct((comps * cols, 2 * cols), jnp.bfloat16),
        jax.ShapeDtypeStruct((comps * rows, 4 * rows), jnp.bfloat16),
        jax.ShapeDtypeStruct((count, rows, cols), residual.dtype),
        jax.ShapeDtypeStruct((count, rows, cols), f32),
    ]
    kept += [jax.ShapeDtypeStruct((slots,), jnp.int32)] * 2
    kept += [jax.ShapeDtypeStruct((count,), jnp.int32)]
    kept += [jax.ShapeDtypeStruct((comps, count), f32)]
    made = pl.pallas_call(
        functools.partial(resample_kernel, cfg, True, chunks[:1], False),
        out_shape=[slab(chunks[0][1]) for _ in range(n)] + kept,
        in_specs=[hbm] * 9,
        out_specs=[vmem] * (n + 4) + [smem] * 4,
        scratch_shapes=[SMEM((count,), jnp.int32)] * 4
        + [VMEM(psf_taps.shape, f32)]
        + [SMEM((epochs,), jnp.int32)] * 2
        + common,
        compiler_params=params,
        name="resample_0",
    )(*inputs)
    slabs, kept = [list(made[:n])], made[n:]
    for k in range(1, len(chunks)):
        last = k == len(chunks) - 1
        made = pl.pallas_call(
            functools.partial(resample_kernel, cfg, False, chunks[k : k + 1], last),
            out_shape=[slab(chunks[k][1]) for _ in range(n)] + [slab(capacity)] * last,
            in_specs=[smem] * 4 + [vmem] * 4,
            out_specs=[vmem] * (n + last),
            scratch_shapes=common,
            compiler_params=params,
        )(*kept[4:], *kept[:4])
        slabs.append(list(made[:n]))
    own = made[-1]

    def turn(x, d):
        return lax.ppermute(x, "epoch", [(i, (i + d) % epochs) for i in range(epochs)])

    def beside(x, d):
        route = [(i, i + d) for i in range(tiles) if 0 <= i + d < tiles]
        return lax.ppermute(x, "tile", route)

    def swap(x, k):
        if not checked:
            return x
        return lax.ppermute(x, "tile", [(i, i ^ (1 << k)) for i in range(tiles)])

    queues = Queues(cfg, chunks, sends)
    sources = [own]
    waves = []
    table = over = None
    for k in range(len(chunks)):
        sources += [turn(slabs[k][d - 1], d) for d in range(1, epochs)]
        out_shape = [slab(sends[k])] * 2
        out_specs = [vmem] * 2
        extra = []
        if k == 0:
            out_shape.append(jax.ShapeDtypeStruct((queues.size,), jnp.int32))
            out_specs.append(smem)
            extra = [SMEM((1, LANES), f32)] * epochs + [pltpu.SemaphoreType.DMA((epochs,))]
        out_shape.append(jax.ShapeDtypeStruct((HEAD, LANES), f32))
        out_specs.append(vmem)
        told = [over, swap(over, k - 1)] if k else []
        result = pl.pallas_call(
            functools.partial(collect_kernel, cfg, queues, k, ends),
            out_shape=out_shape,
            in_specs=([smem] if k else []) + [vmem] * (len(told) + len(sources)),
            out_specs=out_specs,
            scratch_shapes=extra,
            compiler_params=params,
        )(*([table] if k else []), *told, *sources)
        if k == 0:
            table = result[2]
        over = result[-1]
        waves.append([beside(result[0], -1), beside(result[1], 1)])
    early = [x for wave in waves[:-1] for x in wave]
    late = waves[-1]
    total_shape = jax.ShapeDtypeStruct((cells, rows, cols), f32)

    def heads(arrays):
        return [SMEM((1, LANES), f32)] * len(arrays) + [
            pltpu.SemaphoreType.DMA((len(arrays),))
        ]

    total = pl.pallas_call(
        functools.partial(settle_kernel, cfg, queues),
        out_shape=total_shape,
        in_specs=[smem] + [vmem] * (len(sources) + len(early)),
        out_specs=vmem,
        scratch_shapes=heads(early),
        compiler_params=params,
        name="settle",
    )(table, *sources, *early)
    out, failed = pl.pallas_call(
        functools.partial(finish_kernel, rows),
        out_shape=[total_shape, jax.ShapeDtypeStruct((1,), jnp.int32)],
        in_specs=[vmem] * (3 + len(late)),
        out_specs=[vmem, smem],
        scratch_shapes=[
            *[SMEM((1, LANES), f32)] * len(late),
            VMEM((HEAD, LANES), f32),
            SMEM((1, LANES), f32),
            pltpu.SemaphoreType.DMA((len(late) + 1,)),
        ],
        compiler_params=params,
        name="finish",
    )(total, over, swap(over, len(chunks) - 1), *late)
    return out, failed[0] if checked else None


def on_device(tiles, epochs, *args):
    count, rows, cols = args[0].shape[1:]
    capacity = max(2, min(count // 2, 64 // epochs))
    per_dev = PATCHES // epochs
    cfg = (epochs, capacity, per_dev, tiles, count, rows, cols)
    full = [
        (capacity if k == 0 else 0) + (epochs - 1) * size
        for k, (_, size) in enumerate(plan_chunks(capacity))
    ]
    sends = full
    if capacity >= 16 and tiles == 1 << len(full):
        sends = [5 * capacity // 4, 7 * capacity // 8, 3 * capacity // 8]
        sends = [min(a, b) for a, b in zip(sends, full)]
    out, failed = run(cfg, sends, args)
    if failed is not None:

        def again(state):
            return jnp.zeros((), jnp.int32), run(cfg, full, args)[0]

        _, out = lax.while_loop(lambda state: state[0] > 0, again, (failed, out))
    return out.reshape(1, BANDS, per_dev, rows, cols)


def solution(mesh):
    in_specs = (
        P("tile", "epoch", None, None),
        P("tile", "epoch", None, None),
        P("tile", "epoch", None),
        P(),
        P("tile", "epoch", None),
        P("tile", "epoch"),
        P("tile", "epoch"),
        P("tile", "epoch"),
        P("tile", "epoch"),
    )
    out_specs = P("tile", None, "epoch", None, None)
    epochs = mesh.shape["epoch"]
    return jax.shard_map(
        functools.partial(on_device, mesh.shape["tile"], epochs),
        mesh=mesh,
        in_specs=in_specs,
        out_specs=out_specs,
        check_vma=False,
    )
```

```python
import functools

import jax
import jax.numpy as jnp
from jax import lax
from jax.experimental import pallas as pl
from jax.experimental.pallas import tpu as pltpu
from jax.sharding import PartitionSpec as P


BANDS = 6
PATCHES = 32
HEAD = 8
LANES = 128


SMEM = pltpu.SMEM
VMEM = pltpu.VMEM
MIB = 1 << 20


def halves(x):
    high = x.astype(jnp.bfloat16)
    low = (x - high.astype(jnp.float32)).astype(jnp.bfloat16)
    return high, low


def plan_chunks(capacity):
    if capacity >= 16:
        sizes = (capacity // 4, capacity // 2, capacity - capacity // 4 - capacity // 2)
    else:
        sizes = (capacity // 2, capacity - capacity // 2)
    starts = [sum(sizes[:k]) for k in range(len(sizes))]
    return list(zip(starts, sizes))


def head_lanes():
    return lax.broadcasted_iota(jnp.int32, (HEAD, LANES), 1)


def build_bands(taps_ref, cols_ref, rows_ref):
    comps, _, taps = taps_ref.shape
    cols = cols_ref.shape[1] // 2
    rows = rows_ref.shape[1] // 4
    half = (taps - 1) // 2
    tap = lax.broadcasted_iota(jnp.int32, (taps, LANES), 0)
    lane = lax.broadcasted_iota(jnp.int32, (taps, LANES), 1)
    place_col = (lax.rem(lane + tap - half + cols, cols) == 0).astype(jnp.float32)
    place_row = (lax.rem(lane - tap + half + 2 * rows, rows) == 0).astype(jnp.float32)
    base_col = jnp.dot(
        taps_ref[:, 0, :], place_col, precision=lax.Precision.HIGHEST,
        preferred_element_type=jnp.float32,
    )
    base_row = jnp.dot(
        taps_ref[:, 1, :], place_row, precision=lax.Precision.HIGHEST,
        preferred_element_type=jnp.float32,
    )
    up = lax.broadcasted_iota(jnp.int32, (cols, LANES), 0)
    across = lax.broadcasted_iota(jnp.int32, (cols, LANES), 1)
    near_col = jnp.abs(across - up) <= half
    up_row = lax.broadcasted_iota(jnp.int32, (rows, LANES), 0)
    across_row = lax.rem(lax.broadcasted_iota(jnp.int32, (rows, LANES), 1), rows)
    near_row = jnp.abs(across_row - up_row) <= half
    for c in range(comps):
        wide = jnp.broadcast_to(base_col[c : c + 1, :], (cols, LANES))
        wide = pltpu.roll(wide, 0, 1, stride=1, stride_axis=0)
        high, low = halves(jnp.where(near_col, wide, 0.0))
        cols_ref[c * cols : (c + 1) * cols, :] = jnp.concatenate([high, low], axis=1)
        wide = jnp.broadcast_to(base_row[c : c + 1, :], (rows, LANES))
        wide = pltpu.roll(wide, 0, 1, stride=1, stride_axis=0)
        high, low = halves(jnp.where(near_row, wide, 0.0))
        rows_ref[c * rows : (c + 1) * rows, :] = jnp.concatenate([high, low], axis=1)


def fill_slots(cfg, places, block_ref, label_ref, front_ref, back_ref):
    epochs, capacity, per_dev, tiles, count, _, _ = cfg
    cells = BANDS * per_dev
    owner_ref, slot_ref, band_ref, offset_ref = places
    tile = lax.axis_index("tile")
    for e in range(epochs):
        front_ref[e] = e * capacity
        back_ref[e] = (e + 1) * capacity - 1

    for b in range(count):
        off = offset_ref[b]
        target = tile + off - 1
        lands = ((target >= 0) & (target < tiles)).astype(jnp.int32)
        stays = lands * (off == 1).astype(jnp.int32)
        o = owner_ref[b]
        front = front_ref[o]
        back = back_ref[o]
        at = jnp.where(lands == 0, epochs * capacity, jnp.where(off == 1, back, front))
        front_ref[o] = front + lands - stays
        back_ref[o] = back - stays
        block_ref[at] = b
        label_ref[at] = off * cells + band_ref[b] * per_dev + slot_ref[b] + 1


def take(refs, at):
    at = at + 2
    return [*refs[:at], *refs[at + 1 :], refs[at]]


def resample_kernel(cfg, first, parts, join, *refs):
    epochs, capacity, _, _, _, rows, cols = cfg
    slots = epochs * capacity
    n_out = len(parts)
    if join:
        *refs, joined_ref = take(refs, 8 + n_out)
        mine_ref, theirs_ref, *refs = refs
        joined_ref[...] = jnp.maximum(mine_ref[...], theirs_ref[...])
    if first:
        small_hbm, large_hbm, rest = refs[:6], refs[6:9], refs[9:]
        outs, rest = rest[:n_out], rest[n_out:]
        cols_ref, rows_ref, res_ref, inv_ref, block_ref, label_ref = rest[:6]
        shift_ref, coeff_ref, *places, taps_ref, front_ref, back_ref = rest[6:15]
        small = [*places, shift_ref, coeff_ref]
        rest = rest[15:]
        pieces = [
            *zip(small_hbm, small),
            *zip(large_hbm, (taps_ref, res_ref, inv_ref)),
        ]
    else:
        block_ref, label_ref, shift_ref, coeff_ref = refs[:4]
        cols_ref, rows_ref, res_ref, inv_ref = refs[4:8]
        outs, rest = refs[8 : 8 + n_out], refs[8 + n_out :]
        pieces = []
    spread_refs, todo_ref, sems = rest[:2], rest[2], rest[3]
    fetches = [
        pltpu.make_async_copy(src, dst, sems.at[i]) for i, (src, dst) in enumerate(pieces)
    ]
    for fetch in fetches:
        fetch.start()

    if first:
        for i in range(slots):
            label_ref[i] = 0
            block_ref[i] = 0
        for fetch in fetches[:4] + fetches[6:7]:
            fetch.wait()
        build_bands(taps_ref, cols_ref, rows_ref)
        fill_slots(cfg, places, block_ref, label_ref, front_ref, back_ref)

    me = lax.axis_index("epoch")
    total = jnp.int32(0)
    for k, (d, start, size) in enumerate(parts):
        o = lax.rem(me + d, epochs)
        for s in range(size):
            at = o * capacity + start + s
            todo_ref[0, total] = block_ref[at]
            todo_ref[1, total] = k * slots + s
            total = total + (label_ref[at] > 0).astype(jnp.int32)
    for i in range(3):
        todo_ref[0, total + i] = 0
        todo_ref[1, total + i] = len(parts) * slots

    lane = head_lanes()
    if any(start == 0 for _, start, _ in parts):
        head = jnp.zeros((HEAD, LANES), jnp.float32)
        for j in range(slots):
            head = jnp.where(lane == j, label_ref[j].astype(jnp.float32), head)
        for k, (d, start, size) in enumerate(parts):
            if start == 0:
                outs[k][size * rows : size * rows + HEAD, :] = head

    for fetch in fetches[4:6] + fetches[7:]:
        fetch.wait()
    comps = cols_ref.shape[0] // cols
    lanes = lax.broadcasted_iota(jnp.int32, (rows, cols), 1)

    def work(base, twos):
        jobs_here = [(todo_ref[0, base + g], todo_ref[1, base + g]) for g in range(2 * twos)]
        for t in range(twos):
            blocks = [b for b, _ in jobs_here[2 * t : 2 * t + 2]]
            spread_ref = spread_refs[t]
            sides = []
            for b in blocks:
                high, low = halves(inv_ref[b] * res_ref[b].astype(jnp.float32))
                sides.append(jnp.concatenate([high, low, high, low], axis=0))
            down = jnp.dot(
                rows_ref[...],
                jnp.concatenate(sides, axis=1),
                preferred_element_type=jnp.float32,
            )
            for c in range(comps):
                for g in range(2):
                    part = down[c * rows : (c + 1) * rows, g * cols : (g + 1) * cols]
                    high, low = halves(part * coeff_ref[c, blocks[g]])
                    at = slice(c * cols, (c + 1) * cols)
                    spread_ref[g * rows : (g + 1) * rows, at] = high
                    spread_ref[(2 + g) * rows : (3 + g) * rows, at] = low
        images = []
        for t in range(twos):
            both = jnp.dot(
                spread_refs[t][...], cols_ref[...], preferred_element_type=jnp.float32
            )
            for g in range(2):
                b, where = jobs_here[2 * t + g]
                high = both[g * rows : (g + 1) * rows]
                low = both[(2 + g) * rows : (3 + g) * rows]
                image = high[:, :cols] + (high[:, cols:] + low[:, :cols])
                shift = shift_ref[b]
                images.append(jnp.where(lanes >= shift, pltpu.roll(image, shift, 1), 0.0))
        for (_, where), image in zip(jobs_here, images):
            for k in range(len(parts)):

                @pl.when((where >= k * slots) & (where < (k + 1) * slots))
                def _():
                    s = pl.multiple_of((where - k * slots) * rows, rows)
                    outs[k][pl.ds(s, rows), :] = image

    quads = (total + 1) // 4

    def quad(i, carry):
        work(4 * i, 2)
        return carry

    lax.fori_loop(0, quads, quad, 0)

    @pl.when(total > 4 * quads)
    def _():
        work(4 * quads, 1)


def read_heads(sources, head_refs, sems, meanwhile=None):
    copies = [
        pltpu.make_async_copy(src.at[pl.ds(src.shape[0] - HEAD, 1)], dst, sems.at[i])
        for i, (src, dst) in enumerate(zip(sources, head_refs))
    ]
    for copy in copies:
        copy.start()
    if meanwhile is not None:
        meanwhile()
    for copy in copies:
        copy.wait()


PITCH = 1024


class Queues:
    def __init__(self, cfg, chunks, sends):
        epochs, capacity = cfg[:2]
        self.sources = [(0, 0, 0, capacity)] + [
            (k, d, start, size) for k, (start, size) in enumerate(chunks) for d in range(1, epochs)
        ]
        self.slots = epochs * capacity
        self.waves = len(chunks)
        self.ends = 3 * self.slots + 1
        self.limits = self.ends + 3 * len(self.sources)
        self.size = self.limits + 2 * 2 * self.waves
        self.sends = sends
        self.capacity = capacity

    def entry(self, which, i):
        return which * self.slots + i

    def end(self, which, source):
        return self.ends + which * len(self.sources) + source

    def limit(self, side, wave):
        return self.limits + 2 * (side * self.waves + wave)

    def fill(self, table, labels, cells):
        counts = (jnp.int32(0),) * 3
        for at, (k, d, start, size) in enumerate(self.sources):

            def step(j, counts, d=d, start=start):
                label = labels(d, start + j)
                kind = (label > cells).astype(jnp.int32) + (label > 2 * cells).astype(jnp.int32)
                some = label > 0
                n = jnp.where(kind == 0, counts[0], jnp.where(kind == 1, counts[1], counts[2]))
                place = jnp.where(some, kind * self.slots + n, 3 * self.slots)
                table[place] = j * PITCH + label - 1 - kind * cells
                return tuple(
                    c + (some & (kind == w)).astype(jnp.int32) for w, c in enumerate(counts)
                )

            counts = lax.fori_loop(0, size, step, counts)
            for w in range(3):
                table[self.end(w, at)] = counts[w]
        for side, which in enumerate((0, 2)):
            sent = jnp.int32(0)
            for k in range(self.waves):
                last = max(i for i, source in enumerate(self.sources) if source[0] == k)
                table[self.limit(side, k)] = sent
                sent = jnp.minimum(table[self.end(which, last)], sent + self.sends[k])
                table[self.limit(side, k) + 1] = sent


    def overflow(self, heads, cells, ends):
        slot = lax.broadcasted_iota(jnp.int32, (LANES, LANES), 0)
        epoch = lax.broadcasted_iota(jnp.int32, (LANES, LANES), 1)
        mine = lax.div(slot, self.capacity) == epoch
        over = jnp.zeros((HEAD, LANES), jnp.float32)
        for low, high in ((0, cells), (2 * cells, 3 * cells)):
            amount = jnp.zeros((HEAD, LANES), jnp.float32)
            for head in heads:
                amount = amount + jnp.where((head > low) & (head <= high), 1.0, 0.0)
            sent = jnp.zeros((HEAD, LANES), jnp.float32)
            for end, cap in zip(ends, self.sends):
                here = jnp.where(mine & (lax.rem(slot, self.capacity) < end), 1.0, 0.0)
                have = jnp.dot(
                    amount.astype(jnp.bfloat16),
                    here.astype(jnp.bfloat16),
                    preferred_element_type=jnp.float32,
                )
                sent = jnp.minimum(have, sent + cap)
            over = jnp.maximum(over, jnp.where(have > sent, 1.0, 0.0))
        return over


def collect_kernel(cfg, queues, k, ends, *refs):
    epochs, capacity, per_dev, _, _, rows, _ = cfg
    cells = BANDS * per_dev
    known = [i for i, source in enumerate(queues.sources) if source[0] <= k]
    if k == 0:
        sources, rest = refs[: len(known)], refs[len(known) :]
        prev_ref, next_ref, table, over_ref = rest[:4]
        head_refs, sems = rest[4 : 4 + epochs], rest[4 + epochs]
        read_heads(sources, head_refs, sems)
        mine = lax.axis_index("epoch") * capacity
        queues.fill(table, lambda d, j: head_refs[d][0, mine + j].astype(jnp.int32), cells)
        heads = [src[src.shape[0] - HEAD :, :] for src in sources]
        over = jnp.max(queues.overflow(heads, cells, ends), axis=1, keepdims=True)
        over_ref[...] = jnp.broadcast_to(over, over_ref.shape)
    else:
        table, mine_ref, theirs_ref = refs[:3]
        sources, rest = refs[3 : 3 + len(known)], refs[3 + len(known) :]
        prev_ref, next_ref, over_ref = rest
        over_ref[...] = jnp.maximum(mine_ref[...], theirs_ref[...])
    lane = head_lanes()
    cap = queues.sends[k]
    for side, (which, dst) in enumerate(((0, prev_ref), (2, next_ref))):
        first = table[queues.limit(side, k)]
        last = table[queues.limit(side, k) + 1]
        for i, src in zip(known, sources):
            low = table[queues.end(which, i - 1)] if i else 0
            high = table[queues.end(which, i)]

            def step(r, carry, which=which, src=src, dst=dst, first=first):
                j = table[queues.entry(which, r)] // PITCH
                dst[pl.ds(pl.multiple_of((r - first) * rows, rows), rows), :] = src[
                    pl.ds(pl.multiple_of(j * rows, rows), rows), :
                ]
                return carry

            lax.fori_loop(jnp.maximum(low, first), jnp.minimum(high, last), step, 0)

        def mark(r, head, which=which, first=first):
            cell = table[queues.entry(which, r)] % PITCH
            return jnp.where(lane == r - first, cell.astype(jnp.float32), head)

        amount = jnp.where(lane == LANES - 1, (last - first).astype(jnp.float32), 0.0)
        dst[cap * rows : cap * rows + HEAD, :] = lax.fori_loop(first, last, mark, amount)


def add_waves(total_ref, waves, head_refs, rows):
    for src, head in zip(waves, head_refs):

        def step(j, carry, src=src, head=head):
            cell = head[0, j].astype(jnp.int32)
            block = pl.ds(pl.multiple_of(j * rows, rows), rows)
            total_ref[cell] = total_ref[cell] + src[block, :]
            return carry

        lax.fori_loop(0, head[0, LANES - 1].astype(jnp.int32), step, 0)


def settle_kernel(cfg, queues, *refs):
    rows = cfg[5]
    n = len(queues.sources)
    table, over_ref, sources, rest = refs[0], refs[1], refs[2 : 2 + n], refs[2 + n :]
    waves = (len(rest) - 4) // 2
    early, (total_ref, failed_ref) = rest[:waves], rest[waves : waves + 2]
    head_refs, (said_ref, sems) = rest[waves + 2 : -2], rest[-2:]
    say = pltpu.make_async_copy(over_ref.at[pl.ds(0, 1)], said_ref, sems.at[waves])
    say.start()
    total_ref[...] = jnp.zeros_like(total_ref)
    for i, src in enumerate(sources):

        def step(r, carry, src=src):
            entry = table[queues.entry(1, r)]
            cell = entry % PITCH
            block = pl.ds(pl.multiple_of((entry // PITCH) * rows, rows), rows)
            total_ref[cell] = total_ref[cell] + src[block, :]
            return carry

        low = table[queues.end(1, i - 1)] if i else 0
        lax.fori_loop(low, table[queues.end(1, i)], step, 0)
    read_heads(early, head_refs, sems)
    add_waves(total_ref, early, head_refs, rows)
    say.wait()
    failed_ref[0] = (said_ref[0, 0] > 0.0).astype(jnp.int32)


def finish_kernel(rows, *refs):
    waves = (len(refs) - 3) // 2
    total_ref, sources, out_ref = refs[0], refs[1 : 1 + waves], refs[1 + waves]
    head_refs, sems = refs[2 + waves : -1], refs[-1]

    def take_over():
        out_ref[...] = total_ref[...]

    read_heads(sources, head_refs, sems, take_over)
    add_waves(out_ref, sources, head_refs, rows)


def run(cfg, sends, args):
    (
        residual, inv_variance, psf_coeff, psf_taps, patch_owner,
        patch_slot, band_id, tile_offset, col_shift,
    ) = args
    epochs, capacity, per_dev, tiles, count, rows, cols = cfg
    comps = psf_taps.shape[0]
    cells = BANDS * per_dev
    chunks = plan_chunks(capacity)
    ends = [start + size for start, size in chunks]
    n = epochs - 1
    full = [(capacity if k == 0 else 0) + n * size for k, (_, size) in enumerate(chunks)]
    checked = any(cap < most for cap, most in zip(sends, full))
    f32 = jnp.float32
    smem = pl.BlockSpec(memory_space=SMEM)
    vmem = pl.BlockSpec(memory_space=VMEM)
    hbm = pl.BlockSpec(memory_space=pltpu.HBM)

    def slab(slots):
        return jax.ShapeDtypeStruct((slots * rows + HEAD, cols), f32)

    inputs = (
        patch_owner.reshape(count),
        patch_slot.reshape(count),
        band_id.reshape(count),
        tile_offset.reshape(count),
        col_shift.reshape(count),
        psf_coeff[0].T,
        psf_taps,
        residual[0],
        inv_variance[0],
    )
    inputs = tuple(pltpu.with_memory_space_constraint(x, pltpu.HBM) for x in inputs)
    slots = epochs * capacity
    common = [
        *[VMEM((4 * rows, comps * cols), jnp.bfloat16)] * 2,
        SMEM((2, slots + 3), jnp.int32),
        pltpu.SemaphoreType.DMA((9,)),
    ]
    params = pltpu.CompilerParams(vmem_limit_bytes=24 * MIB)
    kept = [
        jax.ShapeDtypeStruct((comps * cols, 2 * cols), jnp.bfloat16),
        jax.ShapeDtypeStruct((comps * rows, 4 * rows), jnp.bfloat16),
        jax.ShapeDtypeStruct((count, rows, cols), residual.dtype),
        jax.ShapeDtypeStruct((count, rows, cols), f32),
    ]
    kept += [jax.ShapeDtypeStruct((slots + 1,), jnp.int32)] * 2
    kept += [jax.ShapeDtypeStruct((count,), jnp.int32)]
    kept += [jax.ShapeDtypeStruct((comps, count), f32)]
    start, size = chunks[0]
    middle = epochs // 2
    made = pl.pallas_call(
        functools.partial(resample_kernel, cfg, True, [(middle, start, size)], False),
        out_shape=[slab(size)] + kept,
        in_specs=[hbm] * 9,
        out_specs=[vmem] * 5 + [smem] * 4,
        scratch_shapes=[SMEM((count,), jnp.int32)] * 4
        + [VMEM(psf_taps.shape, f32)]
        + [SMEM((epochs,), jnp.int32)] * 2
        + common,
        compiler_params=params,
        name="resample_first",
    )(*inputs)
    farthest, kept = made[0], made[1:]

    def more(parts, told=()):
        join = [jax.ShapeDtypeStruct((HEAD, LANES), f32)] if told else []
        return pl.pallas_call(
            functools.partial(resample_kernel, cfg, False, parts, bool(told)),
            out_shape=[slab(size) for _, _, size in parts] + join,
            in_specs=[vmem] * len(told) + [smem] * 4 + [vmem] * 4,
            out_specs=[vmem] * (len(parts) + len(join)),
            scratch_shapes=common,
            compiler_params=params,
        )(*told, *kept[4:], *kept[:4])

    others = [d for d in range(1, epochs) if d != middle]
    made = more([(d, start, size) for d in others])
    slabs = [[dict(zip(others, made)).get(d, farthest) for d in range(1, epochs)]]
    for k in range(1, len(chunks) - 1):
        slabs.append(more([(d, *chunks[k]) for d in range(1, epochs)]))
    own = more([(0, 0, capacity)])[0]

    def turn(x, d):
        return lax.ppermute(x, "epoch", [(i, (i + d) % epochs) for i in range(epochs)])

    def beside(x, d):
        route = [(i, i + d) for i in range(tiles) if 0 <= i + d < tiles]
        return lax.ppermute(x, "tile", route)

    def swap(x, k):
        if not checked:
            return x
        return lax.ppermute(x, "tile", [(i, i ^ (1 << k)) for i in range(tiles)])

    queues = Queues(cfg, chunks, sends)
    sources = [own]
    waves = []
    table = over = None
    for k in range(len(chunks)):
        if k == 1:
            parts = [(d, *chunks[-1]) for d in range(1, epochs)]
            made = more(parts, (over, swap(over, 0)))
            slabs.append(made[:-1])
            over = made[-1]
        sources += [turn(slabs[k][d - 1], d) for d in range(1, epochs)]
        out_shape = [slab(sends[k])] * 2
        out_specs = [vmem] * 2
        extra = []
        if k == 0:
            out_shape.append(jax.ShapeDtypeStruct((queues.size,), jnp.int32))
            out_specs.append(smem)
            extra = [SMEM((1, LANES), f32)] * epochs + [pltpu.SemaphoreType.DMA((epochs,))]
        out_shape.append(jax.ShapeDtypeStruct((HEAD, LANES), f32))
        out_specs.append(vmem)
        told = [over, swap(over, k)] if k else []
        result = pl.pallas_call(
            functools.partial(collect_kernel, cfg, queues, k, ends),
            out_shape=out_shape,
            in_specs=([smem] if k else []) + [vmem] * (len(told) + len(sources)),
            out_specs=out_specs,
            scratch_shapes=extra,
            compiler_params=params,
        )(*([table] if k else []), *told, *sources)
        if k == 0:
            table = result[2]
        over = result[-1]
        waves.append([beside(result[0], -1), beside(result[1], 1)])
    early = waves[0]
    late = [x for wave in waves[1:] for x in wave]
    total_shape = jax.ShapeDtypeStruct((cells, rows, cols), f32)

    def heads(arrays):
        return [SMEM((1, LANES), f32)] * len(arrays)

    total, failed = pl.pallas_call(
        functools.partial(settle_kernel, cfg, queues),
        out_shape=[total_shape, jax.ShapeDtypeStruct((1,), jnp.int32)],
        in_specs=[smem] + [vmem] * (1 + len(sources) + len(early)),
        out_specs=[vmem, smem],
        scratch_shapes=heads(early)
        + [SMEM((1, LANES), f32), pltpu.SemaphoreType.DMA((len(early) + 1,))],
        compiler_params=params,
        name="settle",
    )(table, over, *sources, *early)
    out = pl.pallas_call(
        functools.partial(finish_kernel, rows),
        out_shape=total_shape,
        in_specs=[vmem] * (1 + len(late)),
        out_specs=vmem,
        scratch_shapes=heads(late) + [pltpu.SemaphoreType.DMA((len(late),))],
        compiler_params=params,
        name="finish",
    )(total, *late)
    return out, failed[0] > 0 if checked else None


def on_device(tiles, epochs, *args):
    count, rows, cols = args[0].shape[1:]
    capacity = max(2, min(count // 2, 64 // epochs))
    per_dev = PATCHES // epochs
    cfg = (epochs, capacity, per_dev, tiles, count, rows, cols)
    full = [
        (capacity if k == 0 else 0) + (epochs - 1) * size
        for k, (_, size) in enumerate(plan_chunks(capacity))
    ]
    sends = full
    if capacity >= 16 and tiles == 1 << len(full):
        sends = [7 * capacity // 8, 7 * capacity // 8, 3 * capacity // 8]
        sends = [min(a, b) for a, b in zip(sends, full)]
    out, failed = run(cfg, sends, args)
    if failed is not None:

        def again(state):
            return jnp.zeros((), bool), run(cfg, full, args)[0]

        _, out = lax.while_loop(lambda state: state[0], again, (failed, out))
    return out.reshape(1, BANDS, per_dev, rows, cols)


def solution(mesh):
    in_specs = (
        P("tile", "epoch", None, None),
        P("tile", "epoch", None, None),
        P("tile", "epoch", None),
        P(),
        P("tile", "epoch", None),
        P("tile", "epoch"),
        P("tile", "epoch"),
        P("tile", "epoch"),
        P("tile", "epoch"),
    )
    out_specs = P("tile", None, "epoch", None, None)
    epochs = mesh.shape["epoch"]
    return jax.shard_map(
        functools.partial(on_device, mesh.shape["tile"], epochs),
        mesh=mesh,
        in_specs=in_specs,
        out_specs=out_specs,
        check_vma=False,
    )
```

```python
import functools

import jax
import jax.numpy as jnp
from jax import lax
from jax.experimental import pallas as pl
from jax.experimental.pallas import tpu as pltpu
from jax.sharding import PartitionSpec as P


BANDS = 6
PATCHES = 32
HEAD = 8
LANES = 128


SMEM = pltpu.SMEM
VMEM = pltpu.VMEM
MIB = 1 << 20


def halves(x):
    high = x.astype(jnp.bfloat16)
    low = (x - high.astype(jnp.float32)).astype(jnp.bfloat16)
    return high, low


def plan_chunks(capacity):
    if capacity >= 16:
        sizes = (capacity // 4, capacity // 2, capacity - capacity // 4 - capacity // 2)
    else:
        sizes = (capacity // 2, capacity - capacity // 2)
    starts = [sum(sizes[:k]) for k in range(len(sizes))]
    return list(zip(starts, sizes))


def head_lanes():
    return lax.broadcasted_iota(jnp.int32, (HEAD, LANES), 1)


def build_bands(taps_ref, cols_ref, rows_ref):
    comps, _, taps = taps_ref.shape
    cols = cols_ref.shape[1] // 2
    rows = rows_ref.shape[1] // 4
    half = (taps - 1) // 2
    tap = lax.broadcasted_iota(jnp.int32, (taps, LANES), 0)
    lane = lax.broadcasted_iota(jnp.int32, (taps, LANES), 1)
    place_col = (lax.rem(lane + tap - half + cols, cols) == 0).astype(jnp.float32)
    place_row = (lax.rem(lane - tap + half + 2 * rows, rows) == 0).astype(jnp.float32)
    base_col = jnp.dot(
        taps_ref[:, 0, :], place_col, precision=lax.Precision.HIGHEST,
        preferred_element_type=jnp.float32,
    )
    base_row = jnp.dot(
        taps_ref[:, 1, :], place_row, precision=lax.Precision.HIGHEST,
        preferred_element_type=jnp.float32,
    )
    up = lax.broadcasted_iota(jnp.int32, (cols, LANES), 0)
    across = lax.broadcasted_iota(jnp.int32, (cols, LANES), 1)
    near_col = jnp.abs(across - up) <= half
    up_row = lax.broadcasted_iota(jnp.int32, (rows, LANES), 0)
    across_row = lax.rem(lax.broadcasted_iota(jnp.int32, (rows, LANES), 1), rows)
    near_row = jnp.abs(across_row - up_row) <= half
    for c in range(comps):
        wide = jnp.broadcast_to(base_col[c : c + 1, :], (cols, LANES))
        wide = pltpu.roll(wide, 0, 1, stride=1, stride_axis=0)
        high, low = halves(jnp.where(near_col, wide, 0.0))
        cols_ref[c * cols : (c + 1) * cols, :] = jnp.concatenate([high, low], axis=1)
        wide = jnp.broadcast_to(base_row[c : c + 1, :], (rows, LANES))
        wide = pltpu.roll(wide, 0, 1, stride=1, stride_axis=0)
        high, low = halves(jnp.where(near_row, wide, 0.0))
        rows_ref[c * rows : (c + 1) * rows, :] = jnp.concatenate([high, low], axis=1)


def fill_slots(cfg, places, block_ref, label_ref, front_ref, back_ref):
    epochs, capacity, per_dev, tiles, count, _, _ = cfg
    cells = BANDS * per_dev
    owner_ref, slot_ref, band_ref, offset_ref = places
    tile = lax.axis_index("tile")
    for e in range(epochs):
        front_ref[e] = e * capacity
        back_ref[e] = (e + 1) * capacity - 1

    for b in range(count):
        off = offset_ref[b]
        target = tile + off - 1
        lands = ((target >= 0) & (target < tiles)).astype(jnp.int32)
        stays = lands * (off == 1).astype(jnp.int32)
        o = owner_ref[b]
        front = front_ref[o]
        back = back_ref[o]
        at = jnp.where(lands == 0, epochs * capacity, jnp.where(off == 1, back, front))
        front_ref[o] = front + lands - stays
        back_ref[o] = back - stays
        block_ref[at] = b
        label_ref[at] = off * cells + band_ref[b] * per_dev + slot_ref[b] + 1


def take(refs, at):
    at = at + 2
    return [*refs[:at], *refs[at + 1 :], refs[at]]


def resample_kernel(cfg, first, parts, join, *refs):
    epochs, capacity, _, _, _, rows, cols = cfg
    slots = epochs * capacity
    n_out = len(parts)
    if join:
        *refs, joined_ref = take(refs, 8 + n_out)
        mine_ref, theirs_ref, *refs = refs
        joined_ref[...] = jnp.maximum(mine_ref[...], theirs_ref[...])
    if first:
        small_hbm, large_hbm, rest = refs[:6], refs[6:9], refs[9:]
        outs, rest = rest[:n_out], rest[n_out:]
        cols_ref, rows_ref, res_ref, inv_ref, block_ref, label_ref = rest[:6]
        shift_ref, coeff_ref, *places, taps_ref, front_ref, back_ref = rest[6:15]
        small = [*places, shift_ref, coeff_ref]
        rest = rest[15:]
        pieces = [
            *zip(small_hbm, small),
            *zip(large_hbm, (taps_ref, res_ref, inv_ref)),
        ]
    else:
        block_ref, label_ref, shift_ref, coeff_ref = refs[:4]
        cols_ref, rows_ref, res_ref, inv_ref = refs[4:8]
        outs, rest = refs[8 : 8 + n_out], refs[8 + n_out :]
        pieces = []
    spread_refs, todo_ref, sems = rest[:2], rest[2], rest[3]
    fetches = [
        pltpu.make_async_copy(src, dst, sems.at[i]) for i, (src, dst) in enumerate(pieces)
    ]
    for fetch in fetches:
        fetch.start()

    if first:
        for i in range(slots):
            label_ref[i] = 0
            block_ref[i] = 0
        for fetch in fetches[:4] + fetches[6:7]:
            fetch.wait()
        build_bands(taps_ref, cols_ref, rows_ref)
        fill_slots(cfg, places, block_ref, label_ref, front_ref, back_ref)

    me = lax.axis_index("epoch")
    total = jnp.int32(0)
    for k, (d, start, size) in enumerate(parts):
        o = lax.rem(me + d, epochs)
        for s in range(size):
            at = o * capacity + start + s
            todo_ref[0, total] = block_ref[at]
            todo_ref[1, total] = k * slots + s
            total = total + (label_ref[at] > 0).astype(jnp.int32)
    for i in range(3):
        todo_ref[0, total + i] = 0
        todo_ref[1, total + i] = len(parts) * slots

    lane = head_lanes()
    if any(start == 0 for _, start, _ in parts):
        head = jnp.zeros((HEAD, LANES), jnp.float32)
        for j in range(slots):
            head = jnp.where(lane == j, label_ref[j].astype(jnp.float32), head)
        for k, (d, start, size) in enumerate(parts):
            if start == 0:
                outs[k][size * rows : size * rows + HEAD, :] = head

    for fetch in fetches[4:6] + fetches[7:]:
        fetch.wait()
    comps = cols_ref.shape[0] // cols
    lanes = lax.broadcasted_iota(jnp.int32, (rows, cols), 1)

    def work(base, twos):
        jobs_here = [(todo_ref[0, base + g], todo_ref[1, base + g]) for g in range(2 * twos)]
        for t in range(twos):
            blocks = [b for b, _ in jobs_here[2 * t : 2 * t + 2]]
            spread_ref = spread_refs[t]
            sides = []
            for b in blocks:
                high, low = halves(inv_ref[b] * res_ref[b].astype(jnp.float32))
                sides.append(jnp.concatenate([high, low, high, low], axis=0))
            down = jnp.dot(
                rows_ref[...],
                jnp.concatenate(sides, axis=1),
                preferred_element_type=jnp.float32,
            )
            for c in range(comps):
                for g in range(2):
                    part = down[c * rows : (c + 1) * rows, g * cols : (g + 1) * cols]
                    high, low = halves(part * coeff_ref[c, blocks[g]])
                    at = slice(c * cols, (c + 1) * cols)
                    spread_ref[g * rows : (g + 1) * rows, at] = high
                    spread_ref[(2 + g) * rows : (3 + g) * rows, at] = low
        images = []
        for t in range(twos):
            both = jnp.dot(
                spread_refs[t][...], cols_ref[...], preferred_element_type=jnp.float32
            )
            for g in range(2):
                b, where = jobs_here[2 * t + g]
                high = both[g * rows : (g + 1) * rows]
                low = both[(2 + g) * rows : (3 + g) * rows]
                image = high[:, :cols] + (high[:, cols:] + low[:, :cols])
                shift = shift_ref[b]
                images.append(jnp.where(lanes >= shift, pltpu.roll(image, shift, 1), 0.0))
        for (_, where), image in zip(jobs_here, images):
            for k in range(len(parts)):

                @pl.when((where >= k * slots) & (where < (k + 1) * slots))
                def _():
                    s = pl.multiple_of((where - k * slots) * rows, rows)
                    outs[k][pl.ds(s, rows), :] = image

    quads = (total + 1) // 4

    def quad(i, carry):
        work(4 * i, 2)
        return carry

    lax.fori_loop(0, quads, quad, 0)

    @pl.when(total > 4 * quads)
    def _():
        work(4 * quads, 1)


def read_heads(sources, head_refs, sems):
    copies = [
        pltpu.make_async_copy(src.at[pl.ds(src.shape[0] - HEAD, 1)], dst, sems.at[i])
        for i, (src, dst) in enumerate(zip(sources, head_refs))
    ]
    for copy in copies:
        copy.start()
    for copy in copies:
        copy.wait()


PITCH = 1024


class Queues:
    def __init__(self, cfg, chunks, sends):
        epochs, capacity = cfg[:2]
        self.sources = [(0, 0, 0, capacity)] + [
            (k, d, start, size) for k, (start, size) in enumerate(chunks) for d in range(1, epochs)
        ]
        self.slots = epochs * capacity
        self.waves = len(chunks)
        self.ends = 3 * self.slots + 1
        self.limits = self.ends + 3 * len(self.sources)
        self.size = self.limits + 2 * 2 * self.waves
        self.sends = sends
        self.capacity = capacity

    def entry(self, which, i):
        return which * self.slots + i

    def end(self, which, source):
        return self.ends + which * len(self.sources) + source

    def limit(self, side, wave):
        return self.limits + 2 * (side * self.waves + wave)

    def fill(self, table, labels, cells):
        counts = (jnp.int32(0),) * 3
        for at, (k, d, start, size) in enumerate(self.sources):

            def step(j, counts, d=d, start=start):
                label = labels(d, start + j)
                kind = (label > cells).astype(jnp.int32) + (label > 2 * cells).astype(jnp.int32)
                some = label > 0
                n = jnp.where(kind == 0, counts[0], jnp.where(kind == 1, counts[1], counts[2]))
                place = jnp.where(some, kind * self.slots + n, 3 * self.slots)
                table[place] = j * PITCH + label - 1 - kind * cells
                return tuple(
                    c + (some & (kind == w)).astype(jnp.int32) for w, c in enumerate(counts)
                )

            counts = lax.fori_loop(0, size, step, counts)
            for w in range(3):
                table[self.end(w, at)] = counts[w]
        for side, which in enumerate((0, 2)):
            sent = jnp.int32(0)
            for k in range(self.waves):
                last = max(i for i, source in enumerate(self.sources) if source[0] == k)
                table[self.limit(side, k)] = sent
                sent = jnp.minimum(table[self.end(which, last)], sent + self.sends[k])
                table[self.limit(side, k) + 1] = sent


    def overflow(self, heads, cells, ends):
        slot = lax.broadcasted_iota(jnp.int32, (LANES, LANES), 0)
        epoch = lax.broadcasted_iota(jnp.int32, (LANES, LANES), 1)
        mine = lax.div(slot, self.capacity) == epoch
        over = jnp.zeros((HEAD, LANES), jnp.float32)
        for low, high in ((0, cells), (2 * cells, 3 * cells)):
            amount = jnp.zeros((HEAD, LANES), jnp.float32)
            for head in heads:
                amount = amount + jnp.where((head > low) & (head <= high), 1.0, 0.0)
            sent = jnp.zeros((HEAD, LANES), jnp.float32)
            for end, cap in zip(ends, self.sends):
                here = jnp.where(mine & (lax.rem(slot, self.capacity) < end), 1.0, 0.0)
                have = jnp.dot(
                    amount.astype(jnp.bfloat16),
                    here.astype(jnp.bfloat16),
                    preferred_element_type=jnp.float32,
                )
                sent = jnp.minimum(have, sent + cap)
            over = jnp.maximum(over, jnp.where(have > sent, 1.0, 0.0))
        return over


def collect_kernel(cfg, queues, k, ends, *refs):
    epochs, capacity, per_dev, _, _, rows, _ = cfg
    cells = BANDS * per_dev
    known = [i for i, source in enumerate(queues.sources) if source[0] <= k]
    if k == 0:
        sources, rest = refs[: len(known)], refs[len(known) :]
        prev_ref, next_ref, table, over_ref = rest[:4]
        head_refs, sems = rest[4 : 4 + epochs], rest[4 + epochs]
        read_heads(sources, head_refs, sems)
        mine = lax.axis_index("epoch") * capacity
        queues.fill(table, lambda d, j: head_refs[d][0, mine + j].astype(jnp.int32), cells)
        heads = [src[src.shape[0] - HEAD :, :] for src in sources]
        over = jnp.max(queues.overflow(heads, cells, ends), axis=1, keepdims=True)
        over_ref[...] = jnp.broadcast_to(over, over_ref.shape)
    else:
        table, mine_ref, theirs_ref = refs[:3]
        sources, rest = refs[3 : 3 + len(known)], refs[3 + len(known) :]
        prev_ref, next_ref, over_ref = rest
        over_ref[...] = jnp.maximum(mine_ref[...], theirs_ref[...])
    lane = head_lanes()
    cap = queues.sends[k]
    for side, (which, dst) in enumerate(((0, prev_ref), (2, next_ref))):
        first = table[queues.limit(side, k)]
        last = table[queues.limit(side, k) + 1]
        for i, src in zip(known, sources):
            low = table[queues.end(which, i - 1)] if i else 0
            high = table[queues.end(which, i)]

            def step(r, carry, which=which, src=src, dst=dst, first=first):
                j = table[queues.entry(which, r)] // PITCH
                dst[pl.ds(pl.multiple_of((r - first) * rows, rows), rows), :] = src[
                    pl.ds(pl.multiple_of(j * rows, rows), rows), :
                ]
                return carry

            lax.fori_loop(jnp.maximum(low, first), jnp.minimum(high, last), step, 0)

        def mark(r, head, which=which, first=first):
            cell = table[queues.entry(which, r)] % PITCH
            return jnp.where(lane == r - first, cell.astype(jnp.float32), head)

        amount = jnp.where(lane == LANES - 1, (last - first).astype(jnp.float32), 0.0)
        dst[cap * rows : cap * rows + HEAD, :] = lax.fori_loop(first, last, mark, amount)


def add_waves(total_ref, waves, head_refs, rows):
    for src, head in zip(waves, head_refs):

        def step(j, carry, src=src, head=head):
            cell = head[0, j].astype(jnp.int32)
            block = pl.ds(pl.multiple_of(j * rows, rows), rows)
            total_ref[cell] = total_ref[cell] + src[block, :]
            return carry

        lax.fori_loop(0, head[0, LANES - 1].astype(jnp.int32), step, 0)


def settle_kernel(cfg, queues, *refs):
    rows = cfg[5]
    n = len(queues.sources)
    table, over_ref, sources, rest = refs[0], refs[1], refs[2 : 2 + n], refs[2 + n :]
    waves = (len(rest) - 4) // 2
    early, (total_ref, failed_ref) = rest[:waves], rest[waves : waves + 2]
    head_refs, (said_ref, sems) = rest[waves + 2 : -2], rest[-2:]
    say = pltpu.make_async_copy(over_ref.at[pl.ds(0, 1)], said_ref, sems.at[waves])
    say.start()
    total_ref[...] = jnp.zeros_like(total_ref)
    for i, src in enumerate(sources):

        def step(r, carry, src=src):
            entry = table[queues.entry(1, r)]
            cell = entry % PITCH
            block = pl.ds(pl.multiple_of((entry // PITCH) * rows, rows), rows)
            total_ref[cell] = total_ref[cell] + src[block, :]
            return carry

        low = table[queues.end(1, i - 1)] if i else 0
        lax.fori_loop(low, table[queues.end(1, i)], step, 0)
    read_heads(early, head_refs, sems)
    add_waves(total_ref, early, head_refs, rows)
    say.wait()
    failed_ref[0] = (said_ref[0, 0] > 0.0).astype(jnp.int32)


def finish_kernel(rows, *refs):
    waves = (len(refs) - 3) // 2
    total_ref, sources, out_ref = refs[0], refs[1 : 1 + waves], refs[1 + waves]
    head_refs, sems = refs[2 + waves : -1], refs[-1]
    out_ref[...] = total_ref[...]
    read_heads(sources, head_refs, sems)
    add_waves(out_ref, sources, head_refs, rows)


def run(cfg, sends, args):
    (
        residual, inv_variance, psf_coeff, psf_taps, patch_owner,
        patch_slot, band_id, tile_offset, col_shift,
    ) = args
    epochs, capacity, per_dev, tiles, count, rows, cols = cfg
    comps = psf_taps.shape[0]
    cells = BANDS * per_dev
    chunks = plan_chunks(capacity)
    ends = [start + size for start, size in chunks]
    n = epochs - 1
    full = [(capacity if k == 0 else 0) + n * size for k, (_, size) in enumerate(chunks)]
    checked = any(cap < most for cap, most in zip(sends, full))
    f32 = jnp.float32
    smem = pl.BlockSpec(memory_space=SMEM)
    vmem = pl.BlockSpec(memory_space=VMEM)
    hbm = pl.BlockSpec(memory_space=pltpu.HBM)

    def slab(slots):
        return jax.ShapeDtypeStruct((slots * rows + HEAD, cols), f32)

    inputs = (
        patch_owner.reshape(count),
        patch_slot.reshape(count),
        band_id.reshape(count),
        tile_offset.reshape(count),
        col_shift.reshape(count),
        psf_coeff[0].T,
        psf_taps,
        residual[0],
        inv_variance[0],
    )
    inputs = tuple(pltpu.with_memory_space_constraint(x, pltpu.HBM) for x in inputs)
    slots = epochs * capacity
    common = [
        *[VMEM((4 * rows, comps * cols), jnp.bfloat16)] * 2,
        SMEM((2, slots + 3), jnp.int32),
        pltpu.SemaphoreType.DMA((9,)),
    ]
    params = pltpu.CompilerParams(vmem_limit_bytes=24 * MIB)
    kept = [
        jax.ShapeDtypeStruct((comps * cols, 2 * cols), jnp.bfloat16),
        jax.ShapeDtypeStruct((comps * rows, 4 * rows), jnp.bfloat16),
        jax.ShapeDtypeStruct((count, rows, cols), residual.dtype),
        jax.ShapeDtypeStruct((count, rows, cols), f32),
    ]
    kept += [jax.ShapeDtypeStruct((slots + 1,), jnp.int32)] * 2
    kept += [jax.ShapeDtypeStruct((count,), jnp.int32)]
    kept += [jax.ShapeDtypeStruct((comps, count), f32)]
    start, size = chunks[0]
    middle = epochs // 2
    made = pl.pallas_call(
        functools.partial(resample_kernel, cfg, True, [(middle, start, size)], False),
        out_shape=[slab(size)] + kept,
        in_specs=[hbm] * 9,
        out_specs=[vmem] * 5 + [smem] * 4,
        scratch_shapes=[SMEM((count,), jnp.int32)] * 4
        + [VMEM(psf_taps.shape, f32)]
        + [SMEM((epochs,), jnp.int32)] * 2
        + common,
        compiler_params=params,
        name="resample_first",
    )(*inputs)
    farthest, kept = made[0], made[1:]

    def more(parts, told=()):
        join = [jax.ShapeDtypeStruct((HEAD, LANES), f32)] if told else []
        return pl.pallas_call(
            functools.partial(resample_kernel, cfg, False, parts, bool(told)),
            out_shape=[slab(size) for _, _, size in parts] + join,
            in_specs=[vmem] * len(told) + [smem] * 4 + [vmem] * 4,
            out_specs=[vmem] * (len(parts) + len(join)),
            scratch_shapes=common,
            compiler_params=params,
        )(*told, *kept[4:], *kept[:4])

    others = [d for d in range(1, epochs) if d != middle]
    made = more([(d, start, size) for d in others])
    slabs = [[dict(zip(others, made)).get(d, farthest) for d in range(1, epochs)]]
    for k in range(1, len(chunks) - 1):
        slabs.append(more([(d, *chunks[k]) for d in range(1, epochs)]))
    own = more([(0, 0, capacity)])[0]

    def turn(x, d):
        return lax.ppermute(x, "epoch", [(i, (i + d) % epochs) for i in range(epochs)])

    def beside(x, d):
        route = [(i, i + d) for i in range(tiles) if 0 <= i + d < tiles]
        return lax.ppermute(x, "tile", route)

    def swap(x, k):
        if not checked:
            return x
        return lax.ppermute(x, "tile", [(i, i ^ (1 << k)) for i in range(tiles)])

    queues = Queues(cfg, chunks, sends)
    sources = [own]
    waves = []
    table = over = None
    for k in range(len(chunks)):
        if k == 1:
            parts = [(d, *chunks[-1]) for d in range(1, epochs)]
            made = more(parts, (over, swap(over, 0)))
            slabs.append(made[:-1])
            over = made[-1]
        sources += [turn(slabs[k][d - 1], d) for d in range(1, epochs)]
        out_shape = [slab(sends[k])] * 2
        out_specs = [vmem] * 2
        extra = []
        if k == 0:
            out_shape.append(jax.ShapeDtypeStruct((queues.size,), jnp.int32))
            out_specs.append(smem)
            extra = [SMEM((1, LANES), f32)] * epochs + [pltpu.SemaphoreType.DMA((epochs,))]
        out_shape.append(jax.ShapeDtypeStruct((HEAD, LANES), f32))
        out_specs.append(vmem)
        told = [over, swap(over, k)] if k else []
        result = pl.pallas_call(
            functools.partial(collect_kernel, cfg, queues, k, ends),
            out_shape=out_shape,
            in_specs=([smem] if k else []) + [vmem] * (len(told) + len(sources)),
            out_specs=out_specs,
            scratch_shapes=extra,
            compiler_params=params,
        )(*([table] if k else []), *told, *sources)
        if k == 0:
            table = result[2]
        over = result[-1]
        waves.append([beside(result[0], -1), beside(result[1], 1)])
    early = waves[0]
    late = [x for wave in waves[1:] for x in wave]
    total_shape = jax.ShapeDtypeStruct((cells, rows, cols), f32)

    def heads(arrays):
        return [SMEM((1, LANES), f32)] * len(arrays)

    total, failed = pl.pallas_call(
        functools.partial(settle_kernel, cfg, queues),
        out_shape=[total_shape, jax.ShapeDtypeStruct((1,), jnp.int32)],
        in_specs=[smem] + [vmem] * (1 + len(sources) + len(early)),
        out_specs=[vmem, smem],
        scratch_shapes=heads(early)
        + [SMEM((1, LANES), f32), pltpu.SemaphoreType.DMA((len(early) + 1,))],
        compiler_params=params,
        name="settle",
    )(table, over, *sources, *early)
    out = pl.pallas_call(
        functools.partial(finish_kernel, rows),
        out_shape=total_shape,
        in_specs=[vmem] * (1 + len(late)),
        out_specs=vmem,
        scratch_shapes=heads(late) + [pltpu.SemaphoreType.DMA((len(late),))],
        compiler_params=params,
        name="finish",
    )(total, *late)
    return out, failed[0] > 0 if checked else None


def on_device(tiles, epochs, *args):
    count, rows, cols = args[0].shape[1:]
    capacity = max(2, min(count // 2, 64 // epochs))
    per_dev = PATCHES // epochs
    cfg = (epochs, capacity, per_dev, tiles, count, rows, cols)
    full = [
        (capacity if k == 0 else 0) + (epochs - 1) * size
        for k, (_, size) in enumerate(plan_chunks(capacity))
    ]
    sends = full
    if capacity >= 16 and tiles == 1 << len(full):
        sends = [13 * capacity // 16, 7 * capacity // 8, 3 * capacity // 8]
        sends = [min(a, b) for a, b in zip(sends, full)]
    out, failed = run(cfg, sends, args)
    if failed is not None:

        def again(state):
            return jnp.zeros((), bool), run(cfg, full, args)[0]

        _, out = lax.while_loop(lambda state: state[0], again, (failed, out))
    return out.reshape(1, BANDS, per_dev, rows, cols)


def solution(mesh):
    in_specs = (
        P("tile", "epoch", None, None),
        P("tile", "epoch", None, None),
        P("tile", "epoch", None),
        P(),
        P("tile", "epoch", None),
        P("tile", "epoch"),
        P("tile", "epoch"),
        P("tile", "epoch"),
        P("tile", "epoch"),
    )
    out_specs = P("tile", None, "epoch", None, None)
    epochs = mesh.shape["epoch"]
    return jax.shard_map(
        functools.partial(on_device, mesh.shape["tile"], epochs),
        mesh=mesh,
        in_specs=in_specs,
        out_specs=out_specs,
        check_vma=False,
    )
```
